32 devices in a mesh: slab: 2 (over y), ang: 4 (over z), row: 2 (over x), ch: 2 (over core).
Axes of the slice: x: 2, y: 2, z: 4, core: 2. Of those that a mesh axis runs over, the one named last changes fastest.
Arguments:
- projections: float32 [8, 64, 2048], P(('slab', 'ang'), 'row'), parts along dimension 0, may hold values from -6 to 6
- conv1_weight: float32 [8, 3, 3], P('ch'), may hold values from -2 to 2
- conv1_bias: float32 [8], P('ch'), may hold values from -0.5 to 0.5
- filter_taps: float32 [8, 2048], P('ch'), may hold values from -0.125 to 0.125
- conv2_weight: float32 [8, 3, 3], replicated, may hold values from -0.75 to 0.75
- cotangent: float32 [4, 4, 32, 2048], P(('slab', 'row'), None, ('ang', 'ch')), parts along dimension 0, may hold values from -0.0029296875 to 0.0029296875
Outputs:
- sinogram: float32 [4, 4, 32, 2048], P(('slab', 'row'), None, ('ang', 'ch')), parts along dimension 0
- grad_conv1: float32 [16, 3, 3], P(('slab', 'ch')), parts along dimension 0
- grad_bias: float32 [16], P(('slab', 'ch')), parts along dimension 0
- grad_taps: float32 [16, 2048], P(('slab', 'ch')), parts along dimension 0
- grad_conv2: float32 [16, 3, 3], P(('slab', 'ch')), parts along dimension 0
The draws below stay inside these ranges and needn't reach their ends.
There are 2 independent parts, one for each index of `slab`. The reference program is written for one: setup_inputs(seed, part) draws one part's arguments, and reference() takes and returns one part's arrays. A program takes and returns all parts, laid end to end along the dimension named above; an argument that names none is the same for every part. Nothing has to cross between parts.
All inputs are finite; a program needn't handle non-finite values.
Results may differ from the reference program's by a relative error of at most 0.00028.
Values sent between devices are 32-bit elements; how exact they have to be, the bound alone decides.
A program may use at most 64 MiB of HBM per device.

```python
import jax
import jax.numpy as jnp
from jax import lax

W = 2048
C = 8
RD = 32
A = 4
R = 64
N_ROW = 2


def steps_of(rng, extent, pieces, least, high):
    gain = 1.0
    for dim, shards_of in pieces:
        heights = jax.random.uniform(jax.random.fold_in(jax.random.fold_in(rng, 6), dim), (shards_of,), jnp.float32, least / len(pieces), high / len(pieces))
        gain = gain * jnp.repeat(jnp.exp(heights), extent[dim] // shards_of).reshape((-1,) + (1,) * (len(extent) - 1 - dim))
    return gain


def bell_draw(rng, dims, spread, most, split=(), kind=jnp.bfloat16):
    level = steps_of(rng, dims, split, -0.22, 0.18) if split else 1.0
    drawn = jax.random.normal(rng, dims, jnp.float32) * spread * level
    return jnp.minimum(jnp.maximum(drawn, -most), most).astype(kind)


def setup_inputs(seed: int = 0, part: int = 0) -> dict:
    splits = jax.random.split(jax.random.key(seed), 7)
    part_splits = jax.random.split(jax.random.fold_in(splits[6], part), 7)
    return {
        "projections": bell_draw(part_splits[0], (A, R, W), 1.0, 6.0, ((0, 4), (1, 2)), jnp.float32),
        "conv1_weight": bell_draw(splits[1], (C, 3, 3), 9 ** -0.5, 2.0, ((0, 2),), jnp.float32),
        "conv1_bias": jnp.clip(jax.random.uniform(splits[2], (C,), jnp.float32, -0.5, 0.5) * steps_of(splits[2], (C,), ((0, 2),), -0.4, 0.0), -0.5, 0.5),
        "filter_taps": bell_draw(splits[3], (C, W), W ** -0.5, 0.125, ((0, 2),), jnp.float32),
        "conv2_weight": bell_draw(splits[4], (C, 3, 3), (9 * C) ** -0.5, 0.75, (), jnp.float32),
        "cotangent": bell_draw(part_splits[5], (N_ROW, A, RD, W), 0.0005, 0.0029296875, ((0, 2), (2, 8)), jnp.float32),
    }


def row_shift(source, row_tap, col_tap):
    padded = jnp.pad(source, ((0, 0), (1, 1), (1, 1)))
    return padded[:, row_tap:row_tap + R, col_tap:col_tap + W]


def angle_shift(source, ang_tap, col_tap):
    rolled = jnp.roll(source, 1 - ang_tap, axis=0)
    padded = jnp.pad(rolled, ((0, 0), (0, 0), (1, 1)))
    return padded[:, :, col_tap:col_tap + W]


def reference(projections, conv1_weight, conv1_bias, filter_taps, conv2_weight, cotangent):
    upstream = jnp.transpose(cotangent, (1, 0, 2, 3)).reshape(A, R, W)

    def one_channel(running_sum, weights):
        first_kernel, bias_value, filter_row, second_kernel = weights
        pre_act = jnp.zeros((A, R, W), jnp.float32) + bias_value
        for row_tap in range(3):
            for col_tap in range(3):
                pre_act = pre_act + first_kernel[row_tap, col_tap] * row_shift(projections, row_tap, col_tap)
        gate_value = jax.nn.sigmoid(pre_act)
        hidden = pre_act * gate_value
        spec_hidden = jnp.fft.fft(hidden, axis=-1)
        spec_filter = jnp.fft.fft(filter_row)
        filtered = jnp.real(jnp.fft.ifft(jnp.conj(spec_filter) * spec_hidden, axis=-1)).astype(jnp.float32)
        out_part = jnp.zeros((A, R, W), jnp.float32)
        grad_filtered = jnp.zeros((A, R, W), jnp.float32)
        second_grads = []
        for ang_tap in range(3):
            for col_tap in range(3):
                shifted = angle_shift(filtered, ang_tap, col_tap)
                out_part = out_part + second_kernel[ang_tap, col_tap] * shifted
                second_grads.append(jnp.sum(upstream * shifted))
                grad_filtered = grad_filtered + second_kernel[ang_tap, col_tap] * angle_shift(upstream, 2 - ang_tap, 2 - col_tap)
        spec_back = jnp.fft.fft(grad_filtered, axis=-1)
        grad_hidden = jnp.real(jnp.fft.ifft(spec_filter * spec_back, axis=-1)).astype(jnp.float32)
        cross_spec = jnp.sum(jnp.conj(spec_back) * spec_hidden, axis=(0, 1))
        grad_taps = jnp.real(jnp.fft.ifft(cross_spec)).astype(jnp.float32)
        grad_pre = grad_hidden * gate_value * (1.0 + pre_act * (1.0 - gate_value))
        first_grads = []
        for row_tap in range(3):
            for col_tap in range(3):
                first_grads.append(jnp.sum(grad_pre * row_shift(projections, row_tap, col_tap)))
        grad_bias = jnp.sum(grad_pre)
        return running_sum + out_part, (jnp.stack(first_grads).reshape(3, 3), grad_bias, grad_taps, jnp.stack(second_grads).reshape(3, 3))

    summed, grads = lax.scan(one_channel, jnp.zeros((A, R, W), jnp.float32), (conv1_weight, conv1_bias, filter_taps, conv2_weight))
    sinogram = jnp.transpose(summed.reshape(A, N_ROW, RD, W), (1, 0, 2, 3))
    return (sinogram, grads[0], grads[1], grads[2], grads[3])
```

```python
import functools
import math

import jax
import jax.numpy as jnp
import numpy as np
import ml_dtypes
from jax import lax
from jax.experimental import pallas as pl
from jax.experimental.pallas import tpu as pltpu
from jax.sharding import PartitionSpec as P

MESH = pl.DeviceIdType.MESH
LANES = 128
SLOTS = 32


def twisted(value, k, n, sign):
    re, im = value
    if k == 0:
        return value
    if 4 * k == n:
        return (-im, re) if sign > 0 else (im, -re)
    if 8 * k == n:
        half = math.sqrt(0.5)
        return (half * (re - sign * im), half * (im + sign * re))
    if 8 * k == 3 * n:
        half = math.sqrt(0.5)
        return (half * (-re - sign * im), half * (-im + sign * re))
    cos = math.cos(2 * math.pi * k / n)
    sin = sign * math.sin(2 * math.pi * k / n)
    return (cos * re - sin * im, cos * im + sin * re)


def short_dft(values, sign):
    n = len(values)
    if n == 1:
        return values
    even = short_dft(values[0::2], sign)
    odd = short_dft(values[1::2], sign)
    low, high = [], []
    for k in range(n // 2):
        re, im = twisted(odd[k], k, n, sign)
        low.append((even[k][0] + re, even[k][1] + im))
        high.append((even[k][0] - re, even[k][1] - im))
    return low + high


def split_high_low(table):
    high = table.astype(ml_dtypes.bfloat16)
    low = (table - high.astype(np.float64)).astype(ml_dtypes.bfloat16)
    return high, low


def make_tables(length):
    outer = length // LANES
    index = np.arange(LANES)
    inner = 2 * np.pi * (np.outer(index, index) % LANES) / LANES
    cos, sin = np.cos(inner), np.sin(inner)
    forward = np.block([[cos, -sin], [sin, cos]])
    inverse = np.block([[cos, sin], [-sin, cos]]) / length
    twist = 2 * np.pi * np.outer(np.arange(outer), index) / length
    twist = np.repeat(twist, 8, axis=0)
    tables = np.stack([*split_high_low(forward), *split_high_low(inverse)])
    turns = np.stack([np.cos(twist), np.sin(twist)]).astype(np.float32)
    return tables, turns


def multiply(ref, start, rows, tables_ref, which):
    values = ref[pl.ds(start, rows), :]
    high = values.astype(jnp.bfloat16)
    low = (values - high.astype(jnp.float32)).astype(jnp.bfloat16)
    dot = functools.partial(jnp.dot, preferred_element_type=jnp.float32)
    table_high = tables_ref[which]
    ref[pl.ds(start, rows), :] = (
        dot(high, table_high) + dot(low, table_high) + dot(high, tables_ref[which + 1])
    )


def each(count, body):
    if count <= 32:
        for o in range(1, count):
            body(o)
    else:
        pl.loop(1, count)(body)


def kernel(
    sizes,
    proj_hbm, first_hbm, bias_hbm, taps_hbm, second_hbm, cot_hbm, tables_hbm, turns_hbm,
    sino_ref, first_out_ref, bias_out_ref, taps_out_ref, second_out_ref,
    proj_ref, first_vmem, bias_vmem, taps_ref, cot_ref, tables_ref, turns_ref,
    rows_ref, packed_ref, small_in, small_own,
    got, top, bottom, all_taps, all_packed, first_ref, second_ref,
    cot_shift, proj_shift, spec_back, spec_hidden, spec_taps, work,
    back, slope, filt, partial, mixed,
    outgoing, incoming, collected,
    rows_send, rows_recv, edge_send, edge_recv, taps_send, taps_recv,
    packed_send, packed_recv, sum_send, sum_recv, gather_send, gather_recv, small_send, small_recv, load_sem, local_sem,
):
    ang_n, row_n, ch_n = sizes
    n = ang_n * row_n * ch_n
    angles, rq, columns = cot_ref.shape
    chans = second_ref.shape[2]
    chans_dev = taps_ref.shape[0]
    held = proj_ref.shape[0]
    both = angles * rq
    half = both // 2
    outer = columns // LANES
    block = outer * half
    slab = lax.axis_index("slab")
    z, k, c0 = lax.axis_index("ang"), lax.axis_index("row"), lax.axis_index("ch")
    me = (z * row_n + k) * ch_n + c0

    def partner(o):
        oz, ok, oc = o // (row_n * ch_n), o // ch_n % row_n, o % ch_n
        return (z + oz) % ang_n, (k + ok) % row_n, (c0 + oc) % ch_n

    def number(at):
        return (at[0] * row_n + at[1]) * ch_n + at[2]

    barrier = pltpu.get_barrier_semaphore()
    each(n, lambda o: pl.semaphore_signal(
        barrier, inc=1, device_id=(slab, *partner(o)), device_id_type=MESH))

    loads = [
        pltpu.make_async_copy(source, target, load_sem.at[at])
        for at, (source, target) in enumerate((
            (proj_hbm, proj_ref), (first_hbm, first_vmem), (bias_hbm, bias_vmem),
            (taps_hbm, taps_ref), (cot_hbm, cot_ref), (tables_hbm, tables_ref),
            (turns_hbm, turns_ref), (second_hbm, second_ref)))
    ]
    for load in loads:
        load.start()

    def cols(m):
        return slice(m * LANES, (m + 1) * LANES)

    edge = jnp.zeros((outer, LANES), jnp.float32)
    rows_ref[0:outer, :] = edge
    rows_ref[(held + 1) * outer : (held + 2) * outer, :] = edge
    packed_ref[...] = jnp.zeros(packed_ref.shape, jnp.float32)
    loads[0].wait()
    for at in range(0, held, 8):
        for m in range(outer):
            rows_ref[pl.ds((at + 1) * outer + m, 8, stride=outer), :] = proj_ref[at : at + 8, cols(m)]
    loads[1].wait()
    loads[2].wait()
    for i in range(3):
        packed_ref[:, 3 * i : 3 * i + 3] = first_vmem[i]
    for l in range(chans_dev):
        packed_ref[l : l + 1, 9:10] = bias_vmem[0:1, l : l + 1]
    loads[3].wait()
    pl.semaphore_wait(barrier, n - 1)

    def rows_copy(o, slot, target):
        start = pl.multiple_of((target * ch_n + c0) * rq * outer, outer)
        return pltpu.make_async_remote_copy(
            src_ref=rows_ref.at[pl.ds(start, (rq + 2) * outer)], dst_ref=got.at[slot],
            send_sem=rows_send.at[o], recv_sem=rows_recv.at[slot],
            device_id=(slab, target, k, c0), device_id_type=MESH)

    def taps_copy(o, slot, target):
        return pltpu.make_async_remote_copy(
            src_ref=taps_ref, dst_ref=all_taps.at[slot],
            send_sem=taps_send.at[o], recv_sem=taps_recv.at[slot],
            device_id=(slab, z, k, target), device_id_type=MESH)

    def packed_copy(o, slot, target):
        return pltpu.make_async_remote_copy(
            src_ref=packed_ref, dst_ref=all_packed.at[slot],
            send_sem=packed_send.at[o], recv_sem=packed_recv.at[slot],
            device_id=(slab, z, k, target), device_id_type=MESH)

    def top_copy(slot):
        return pltpu.make_async_remote_copy(
            src_ref=rows_ref.at[pl.ds(held * outer, outer)], dst_ref=top.at[slot],
            send_sem=edge_send.at[0], recv_sem=edge_recv.at[0, slot],
            device_id=(slab, 0, (k + 1) % row_n, 0), device_id_type=MESH)

    def bottom_copy(slot):
        return pltpu.make_async_remote_copy(
            src_ref=rows_ref.at[pl.ds(outer, outer)], dst_ref=bottom.at[slot],
            send_sem=edge_send.at[1], recv_sem=edge_recv.at[1, slot],
            device_id=(slab, ang_n - 1, (k + row_n - 1) % row_n, ch_n - 1), device_id_type=MESH)

    for o in range(1, ch_n):
        taps_copy(o, c0, (c0 + o) % ch_n).start()
        packed_copy(o, c0, (c0 + o) % ch_n).start()
    sends_top = jnp.logical_and(c0 == 0, k < row_n - 1)
    sends_bottom = jnp.logical_and(c0 == ch_n - 1, k > 0)

    @pl.when(sends_top)
    def _():
        top_copy(z).start()

    @pl.when(sends_bottom)
    def _():
        bottom_copy(z).start()

    for o in range(1, ang_n):
        rows_copy(o, z, (z + o) % ang_n).start()

    mine_at = pl.multiple_of((z * ch_n + c0) * rq * outer, outer)
    got[z] = rows_ref[pl.ds(mine_at, (rq + 2) * outer), :]
    all_taps[c0] = taps_ref[...]
    all_packed[c0] = packed_ref[...]

    column = lax.broadcasted_iota(jnp.int32, (both, columns), 1)
    first_col, last_col = column == 0, column == columns - 1

    def from_left(x):
        return jnp.where(first_col, 0.0, pltpu.roll(x, 1, 1))

    def from_right(x):
        return jnp.where(last_col, 0.0, pltpu.roll(x, columns - 1, 1))

    lo, hi = slice(0, half), slice(half, both)
    re_l, im_l = slice(0, LANES), slice(LANES, 2 * LANES)

    loads[4].wait()
    upstream = jnp.concatenate([cot_ref[a] for a in range(angles)], axis=0)
    for i in range(3):
        shift = (i - 1) * rq % both
        turned = pltpu.roll(upstream, shift, 0) if shift else upstream
        cot_shift[3 * i] = from_right(turned)
        cot_shift[3 * i + 1] = turned
        cot_shift[3 * i + 2] = from_left(turned)

    def store_forward(ref, start, values):
        for q, (re, im) in enumerate(short_dft(values, -1)):
            part = slice(q * half, (q + 1) * half)
            cos, sin = turns_ref[0, part, :], turns_ref[1, part, :]
            rows = pl.ds(start + q * half, half)
            ref[rows, re_l] = re * cos + im * sin
            ref[rows, im_l] = im * cos - re * sin

    def load_inverse(ref, start):
        values = []
        for q in range(outer):
            part = slice(q * half, (q + 1) * half)
            cos, sin = turns_ref[0, part, :], turns_ref[1, part, :]
            rows = pl.ds(start + q * half, half)
            re, im = ref[rows, re_l], ref[rows, im_l]
            values.append((re * cos - im * sin, im * cos + re * sin))
        return short_dft(values, 1)

    def start_of(c):
        return pl.multiple_of(c * block, block)

    loads[5].wait()
    loads[6].wait()
    loads[7].wait()

    @pl.loop(0, chans)
    def _(c):
        weights = [second_ref[t // 3, t % 3, c] for t in range(9)]
        values = []
        for m in range(outer):
            pair = []
            for rows in (lo, hi):
                total = weights[0] * cot_shift[0, rows, cols(m)]
                for t in range(1, 9):
                    total = total + weights[t] * cot_shift[t, rows, cols(m)]
                pair.append(total)
            values.append(tuple(pair))
        store_forward(spec_back, start_of(c), values)

    step = 4 * block
    for s in range(0, chans * block, step):
        multiply(spec_back, s, step, tables_ref, 0)

    for o in range(1, ch_n):
        source = (c0 + o) % ch_n
        taps_copy(o, source, source).wait_recv()
        packed_copy(o, source, source).wait_recv()
    load_weights = pltpu.make_async_copy(all_packed, first_ref, local_sem)
    load_weights.start()
    taps = jnp.concatenate([all_taps[h] for h in range(ch_n)], axis=0)
    zero = jnp.zeros((chans, LANES), jnp.float32)
    store_forward(spec_taps, 0, [(taps[:, cols(m)], zero) for m in range(outer)])
    multiply(spec_taps, 0, block, tables_ref, 0)

    def tap_row(q, c):
        row = spec_taps[pl.ds(q * half + c, 1), :]
        row = jnp.broadcast_to(row, (half, 2 * LANES))
        return row[:, re_l], row[:, im_l]

    @pl.loop(0, chans)
    def _(c):
        for q in range(outer):
            tr, ti = tap_row(q, c)
            rows = pl.ds(start_of(c) + q * half, half)
            gr, gi = spec_back[rows, re_l], spec_back[rows, im_l]
            work[rows, re_l] = tr * gr - ti * gi
            work[rows, im_l] = tr * gi + ti * gr

    for s in range(0, chans * block, step):
        multiply(work, s, step, tables_ref, 2)

    @pl.loop(0, chans)
    def _(c):
        for m, (re, im) in enumerate(load_inverse(work, start_of(c))):
            back[c, lo, cols(m)] = re
            back[c, hi, cols(m)] = im

    load_weights.wait()
    for o in range(1, ang_n):
        source = (z + o) % ang_n
        rows_copy(o, source, source).wait_recv()

    @pl.when(jnp.logical_and(jnp.logical_and(z == 0, c0 == 0), k > 0))
    def _():
        for a in range(ang_n):
            top_copy(a).wait_recv()
            got[a, 0:outer, :] = top[a]

    @pl.when(jnp.logical_and(jnp.logical_and(z == ang_n - 1, c0 == ch_n - 1), k < row_n - 1))
    def _():
        for a in range(ang_n):
            bottom_copy(a).wait_recv()
            got[a, (rq + 1) * outer : (rq + 2) * outer, :] = bottom[a]

    for a in range(angles):
        for i in range(3):
            for m in range(outer):
                lines = got[a, pl.ds(i * outer + m, rq, stride=outer), :]
                proj_shift[3 * i + 1, a * rq : (a + 1) * rq, cols(m)] = lines
    for i in range(3):
        centre = proj_shift[3 * i + 1]
        proj_shift[3 * i] = from_left(centre)
        proj_shift[3 * i + 2] = from_right(centre)

    @pl.loop(0, chans)
    def _(c):
        h, l = c // chans_dev, c % chans_dev
        weights = [first_ref[h, l, t] for t in range(10)]
        values = []
        for m in range(outer):
            pair = []
            for rows in (lo, hi):
                pre = weights[9] + weights[0] * proj_shift[0, rows, cols(m)]
                for t in range(1, 9):
                    pre = pre + weights[t] * proj_shift[t, rows, cols(m)]
                gate = 0.5 + 0.5 * jnp.tanh(0.5 * pre)
                slope[c, rows, cols(m)] = gate * (1.0 + pre * (1.0 - gate))
                pair.append(pre * gate)
            values.append(tuple(pair))
        store_forward(spec_hidden, start_of(c), values)

    for s in range(0, chans * block, step):
        multiply(spec_hidden, s, step, tables_ref, 0)
    work[pl.ds(chans * block, block), :] = jnp.zeros((block, 2 * LANES), jnp.float32)
    line_of = lax.broadcasted_iota(jnp.int32, (half, LANES), 0)

    def folded(value):
        return jnp.sum(value, axis=0, keepdims=True)


    @pl.loop(0, chans)
    def _(c):
        for q in range(outer):
            tr, ti = tap_row(q, c)
            rows = pl.ds(start_of(c) + q * half, half)
            gr, gi = spec_back[rows, re_l], spec_back[rows, im_l]
            hr, hi_ = spec_hidden[rows, re_l], spec_hidden[rows, im_l]
            work[rows, re_l] = tr * hr + ti * hi_
            work[rows, im_l] = tr * hi_ - ti * hr
            at = slice(chans * block + q * half, chans * block + (q + 1) * half)
            work[at, re_l] = jnp.where(line_of == c, folded(gr * hr + gi * hi_), work[at, re_l])
            work[at, im_l] = jnp.where(line_of == c, folded(gr * hi_ - gi * hr), work[at, im_l])

    multiply(work, chans * block, block, tables_ref, 2)
    for m, (re, im) in enumerate(load_inverse(work, chans * block)):
        outgoing[m] = re

    def sum_copy(o):
        target = partner(o)
        return pltpu.make_async_remote_copy(
            src_ref=outgoing.at[number(target) % outer], dst_ref=incoming.at[o],
            send_sem=sum_send.at[o], recv_sem=sum_recv.at[o],
            device_id=(slab, *target), device_id_type=MESH)

    each(n, lambda o: sum_copy(o).start())
    incoming[0] = outgoing[me % outer]
    partial[...] = jnp.zeros(partial.shape, jnp.float32)

    @pl.loop(0, chans)
    def _(c):
        sums = [jnp.zeros((half, LANES), jnp.float32) for _ in range(10)]
        for m in range(outer):
            for rows in (lo, hi):
                grad = back[c, rows, cols(m)] * slope[c, rows, cols(m)]
                for t in range(9):
                    sums[t] = sums[t] + grad * proj_shift[t, rows, cols(m)]
                sums[9] = sums[9] + grad
        for t in range(10):
            partial[c, t : t + 1, :] = folded(sums[t])

    for s in range(0, chans * block, step):
        multiply(work, s, step, tables_ref, 2)

    @pl.loop(0, chans)
    def _(c):
        sums = [jnp.zeros((half, LANES), jnp.float32) for _ in range(9)]
        for m, (re, im) in enumerate(load_inverse(work, start_of(c))):
            filt[c, lo, cols(m)] = re
            filt[c, hi, cols(m)] = im
            for t in range(9):
                sums[t] = sums[t] + re * cot_shift[t, lo, cols(m)] + im * cot_shift[t, hi, cols(m)]
        for t in range(9):
            partial[c, 16 + t : 17 + t, :] = folded(sums[t])

    small = lax.dot_general(
        jnp.ones((8, LANES), jnp.float32), partial[...].reshape(chans * SLOTS, LANES),
        (((1,), (1,)), ((), ())),
        precision=lax.Precision.HIGHEST, preferred_element_type=jnp.float32)
    width = chans_dev * SLOTS
    for h in range(ch_n):
        small_own[h] = small[0:1, h * width : (h + 1) * width]

    def small_copy(o):
        target = partner(o)
        return pltpu.make_async_remote_copy(
            src_ref=small_own.at[target[2]], dst_ref=small_in.at[me],
            send_sem=small_send.at[o], recv_sem=small_recv.at[o],
            device_id=(slab, *target), device_id_type=MESH)

    each(n, lambda o: small_copy(o).start())
    small_in[me] = small_own[c0]
    each(n, lambda o: sum_copy(o).wait_recv())

    total = incoming[0]
    for d in range(1, n):
        total = total + incoming[d]
    mine = me % outer
    group = me - mine
    for h in range(ch_n):
        collected[mine, h] = total[h * chans_dev : (h + 1) * chans_dev]

    def gather_copy(o):
        target = group + (mine + o) % outer
        to = (target // (row_n * ch_n), target // ch_n % row_n, target % ch_n)
        return pltpu.make_async_remote_copy(
            src_ref=collected.at[mine, to[2]], dst_ref=collected.at[mine, to[2]],
            send_sem=gather_send.at[o], recv_sem=gather_recv.at[o],
            device_id=(slab, *to), device_id_type=MESH)

    each(outer, lambda o: gather_copy(o).start())

    @pl.loop(0, outer)
    def _(m):
        at = pl.ds(pl.multiple_of(m * LANES, LANES), LANES)
        for rows in (lo, hi):
            pieces = [filt[c, rows, at] for c in range(chans)]
            for t in range(9):
                total = second_ref[t // 3, t % 3, 0] * pieces[0]
                for c in range(1, chans):
                    total = total + second_ref[t // 3, t % 3, c] * pieces[c]
                mixed[t, rows, at] = total

    sides = []
    for j in range(3):
        total = mixed[3 + j]
        for i in (0, 2):
            total = total + pltpu.roll(mixed[3 * i + j], -(i - 1) * rq % both, 0)
        sides.append(total)
    image = sides[1] + from_left(sides[0]) + from_right(sides[2])
    for a in range(angles):
        sino_ref[a] = image[a * rq : (a + 1) * rq]

    each(n, lambda o: small_copy(o).wait_recv())

    sums = small_in[0]
    for d in range(1, n):
        sums = sums + small_in[d]
    for l in range(chans_dev):
        for i in range(3):
            at = l * SLOTS + 3 * i
            first_out_ref[i, l : l + 1, :] = sums[:, at : at + 3]
            second_out_ref[i, l : l + 1, :] = sums[:, at + 16 : at + 19]
        bias_out_ref[0:1, l : l + 1] = sums[:, l * SLOTS + 9 : l * SLOTS + 10]

    each(outer, lambda o: gather_copy(o).wait_recv())
    for m in range(outer):
        taps_out_ref[:, cols(m)] = collected[m, c0]

    for o in range(1, ang_n):
        rows_copy(o, z, (z + o) % ang_n).wait_send()
    for o in range(1, ch_n):
        taps_copy(o, c0, (c0 + o) % ch_n).wait_send()
        packed_copy(o, c0, (c0 + o) % ch_n).wait_send()

    @pl.when(sends_top)
    def _():
        top_copy(z).wait_send()

    @pl.when(sends_bottom)
    def _():
        bottom_copy(z).wait_send()

    each(n, lambda o: sum_copy(o).wait_send())
    each(n, lambda o: small_copy(o).wait_send())
    each(outer, lambda o: gather_copy(o).wait_send())


def deliver(*refs):
    count = (len(refs) - 1) // 2
    sources, targets, sems = refs[:count], refs[count : 2 * count], refs[-1]
    copies = [pltpu.make_async_copy(sources[at], targets[at], sems.at[at]) for at in range(count)]
    for copy in copies:
        copy.start()
    for copy in copies:
        copy.wait()


def on_device(sizes, tables, projections, conv1_weight, conv1_bias, filter_taps, conv2_weight, cotangent):
    ang_n, row_n, ch_n = sizes
    n = ang_n * row_n * ch_n
    _, held, columns = projections.shape
    chans_dev = conv1_weight.shape[0]
    chans = chans_dev * ch_n
    _, angles, rq, _ = cotangent.shape
    outer = columns // LANES
    both = angles * rq
    block = outer * both // 2
    f32 = jnp.float32
    vmem = pl.BlockSpec(memory_space=pltpu.VMEM)
    hbm = pl.BlockSpec(memory_space=pltpu.HBM)
    dma = pltpu.SemaphoreType.DMA
    wide = (both, columns)
    shapes = (
        jax.ShapeDtypeStruct((angles, rq, columns), f32),
        jax.ShapeDtypeStruct((3, chans_dev, 3), f32),
        jax.ShapeDtypeStruct((1, chans_dev), f32),
        jax.ShapeDtypeStruct((chans_dev, columns), f32),
        jax.ShapeDtypeStruct((3, chans_dev, 3), f32),
    )
    results = pl.pallas_call(
        functools.partial(kernel, sizes),
        out_shape=tuple(pltpu.VMEM(leaf.shape, f32) for leaf in shapes),
        in_specs=[hbm] * 8,
        out_specs=(vmem,) * 5,
        scratch_shapes=[
            pltpu.VMEM((held, columns), f32),
            pltpu.VMEM((3, chans_dev, 3), f32),
            pltpu.VMEM((1, chans_dev), f32),
            pltpu.VMEM((chans_dev, columns), f32),
            pltpu.VMEM((angles, rq, columns), f32),
            pltpu.VMEM(tables[0].shape, jnp.bfloat16),
            pltpu.VMEM(tables[1].shape, f32),
            pltpu.VMEM(((held + 2) * outer, LANES), f32),
            pltpu.VMEM((chans_dev, LANES), f32),
            pltpu.VMEM((n, 1, LANES), f32),
            pltpu.VMEM((ch_n, 1, LANES), f32),
            pltpu.VMEM((ang_n, (rq + 2) * outer, LANES), f32),
            pltpu.VMEM((ang_n, outer, LANES), f32),
            pltpu.VMEM((ang_n, outer, LANES), f32),
            pltpu.VMEM((ch_n, chans_dev, columns), f32),
            pltpu.VMEM((ch_n, chans_dev, LANES), f32),
            pltpu.SMEM((ch_n, chans_dev, LANES), f32),
            pltpu.SMEM((3, 3, chans), f32),
            pltpu.VMEM((9,) + wide, f32),
            pltpu.VMEM((9,) + wide, f32),
            pltpu.VMEM((chans * block, 2 * LANES), f32),
            pltpu.VMEM((chans * block, 2 * LANES), f32),
            pltpu.VMEM((block, 2 * LANES), f32),
            pltpu.VMEM(((chans + 1) * block, 2 * LANES), f32),
            pltpu.VMEM((chans,) + wide, f32),
            pltpu.VMEM((chans,) + wide, f32),
            pltpu.VMEM((chans,) + wide, f32),
            pltpu.VMEM((chans, SLOTS, LANES), f32),
            pltpu.VMEM((9,) + wide, f32),
            pltpu.VMEM((outer, chans, LANES), f32),
            pltpu.VMEM((n, chans, LANES), f32),
            pltpu.VMEM((outer, ch_n, chans_dev, LANES), f32),
            dma((ang_n,)), dma((ang_n,)), dma((2,)), dma((2, ang_n)),
            dma((ch_n,)), dma((ch_n,)), dma((ch_n,)), dma((ch_n,)),
            dma((n,)), dma((n,)), dma((outer,)), dma((outer,)),
            dma((n,)), dma((n,)), dma((8,)), dma(()),
        ],
        compiler_params=pltpu.CompilerParams(
            collective_id=0, has_side_effects=True, vmem_limit_bytes=63 * 2**20
        ),
        name="tomography",
    )(
        projections[0], jnp.transpose(conv1_weight, (1, 0, 2)), conv1_bias[None], filter_taps,
        jnp.transpose(conv2_weight, (1, 2, 0)), cotangent[0], *tables,
    )
    image, first, bias, taps_out, second = pl.pallas_call(
        deliver,
        out_shape=shapes,
        in_specs=[vmem] * 5,
        out_specs=(hbm,) * 5,
        scratch_shapes=[dma((5,))],
        name="deliver",
    )(*[pltpu.with_memory_space_constraint(leaf, pltpu.VMEM) for leaf in results])
    return (
        image[None], jnp.transpose(first, (1, 0, 2)), bias[0], taps_out,
        jnp.transpose(second, (1, 0, 2)),
    )


def solution(mesh):
    sizes = tuple(mesh.shape[axis] for axis in ("ang", "row", "ch"))

    def whole(projections, conv1_weight, conv1_bias, filter_taps, conv2_weight, cotangent):
        tables = make_tables(projections.shape[-1])

        def local(*arrays):
            return on_device(sizes, tuple(jnp.asarray(t) for t in tables), *arrays)

        return jax.shard_map(
            local,
            mesh=mesh,
            in_specs=(
                P(("slab", "ang"), "row", None),
                P("ch", None, None),
                P("ch"),
                P("ch", None),
                P(),
                P(("slab", "row"), None, ("ang", "ch"), None),
            ),
            out_specs=(
                P(("slab", "row"), None, ("ang", "ch"), None),
                P(("slab", "ch"), None, None),
                P(("slab", "ch")),
                P(("slab", "ch"), None),
                P(("slab", "ch"), None, None),
            ),
            check_vma=False,
        )(projections, conv1_weight, conv1_bias, filter_taps, conv2_weight, cotangent)

    return whole
```

```python
import functools
import math

import jax
import jax.numpy as jnp
import numpy as np
import ml_dtypes
from jax import lax
from jax.experimental import pallas as pl
from jax.experimental.pallas import tpu as pltpu
from jax.sharding import PartitionSpec as P

MESH = pl.DeviceIdType.MESH
LANES = 128
SLOTS = 32


def twisted(value, k, n, sign):
    re, im = value
    if k == 0:
        return value
    if 4 * k == n:
        return (-im, re) if sign > 0 else (im, -re)
    if 8 * k == n:
        half = math.sqrt(0.5)
        return (half * (re - sign * im), half * (im + sign * re))
    if 8 * k == 3 * n:
        half = math.sqrt(0.5)
        return (half * (-re - sign * im), half * (-im + sign * re))
    cos = math.cos(2 * math.pi * k / n)
    sin = sign * math.sin(2 * math.pi * k / n)
    return (cos * re - sin * im, cos * im + sin * re)


def short_dft(values, sign):
    n = len(values)
    if n == 1:
        return values
    even = short_dft(values[0::2], sign)
    odd = short_dft(values[1::2], sign)
    low, high = [], []
    for k in range(n // 2):
        re, im = twisted(odd[k], k, n, sign)
        low.append((even[k][0] + re, even[k][1] + im))
        high.append((even[k][0] - re, even[k][1] - im))
    return low + high


def split_high_low(table):
    high = table.astype(ml_dtypes.bfloat16)
    low = (table - high.astype(np.float64)).astype(ml_dtypes.bfloat16)
    return high, low


def make_tables(length):
    outer = length // LANES
    index = np.arange(LANES)
    inner = 2 * np.pi * (np.outer(index, index) % LANES) / LANES
    cos, sin = np.cos(inner), np.sin(inner)
    forward = np.block([[cos, -sin], [sin, cos]])
    inverse = np.block([[cos, sin], [-sin, cos]]) / length
    twist = 2 * np.pi * np.outer(np.arange(outer), index) / length
    twist = np.repeat(twist, 8, axis=0)
    tables = np.stack([*split_high_low(forward), *split_high_low(inverse)])
    turns = np.stack([np.cos(twist), np.sin(twist)]).astype(np.float32)
    return tables, turns


def padded_rows(rq):
    return -(-(rq + 3) // 8) * 8


def make_masks(angles, rq):
    rp = padded_rows(rq)
    masks = np.zeros((11, angles, rq, angles, 2, 3, rp), np.float32)
    for a in range(angles):
        for r in range(rq):
            for t in range(9):
                masks[t, a, r, a, :, t % 3, r + t // 3] = 1
            masks[9, a, r, a, 0, 1, rq + 2] = 1
            masks[10, a, r, :, 0] = 1
    return masks.reshape(11, angles * rq, angles * 6 * rp)


def fold_rows(values):
    count = len(values)
    line = lax.broadcasted_iota(jnp.int32, values[0].shape, 0)
    step = count // 2
    while step:
        first = (line & step) == 0
        values = [
            jnp.where(first, a, b)
            + jnp.where(first, pltpu.roll(a, count - step, 0), pltpu.roll(b, step, 0))
            for a, b in zip(values[:step], values[step:])
        ]
        step //= 2
    return values[0]


def multiply(ref, start, rows, tables_ref, which):
    values = ref[pl.ds(start, rows), :]
    high = values.astype(jnp.bfloat16)
    low = (values - high.astype(jnp.float32)).astype(jnp.bfloat16)
    dot = functools.partial(jnp.dot, preferred_element_type=jnp.float32)
    table_high = tables_ref[which]
    ref[pl.ds(start, rows), :] = (
        dot(high, table_high) + dot(low, table_high) + dot(high, tables_ref[which + 1])
    )


def team_sizes(sizes):
    return tuple(2 if size % 2 == 0 else 1 for size in sizes[:2])


def each(count, body):
    if count <= 32:
        for o in range(1, count):
            body(o)
    else:
        pl.loop(1, count)(body)


def kernel(
    sizes,
    proj_hbm, first_hbm, bias_hbm, taps_hbm, second_hbm, cot_hbm, tables_hbm, turns_hbm, masks_hbm,
    sino_ref, first_out_ref, bias_out_ref, taps_out_ref, second_out_ref,
    proj_ref, first_vmem, bias_vmem, taps_ref, cot_ref, tables_ref, turns_ref, masks_ref,
    rows_ref, packed_ref, small_own,
    got, top, bottom, all_taps, all_packed, first_ref, second_ref,
    cot_shift, proj_shift, spec_back, spec_hidden, spec_taps, work,
    back, hidden_ref, gate_ref, filt, partial, mixed, lines_ref, first_matrix,
    outgoing, incoming, spread, gathered,
    rows_send, rows_recv, edge_send, edge_recv, taps_send, taps_recv,
    packed_send, packed_recv, sum_send, sum_recv, gather_send, gather_recv, load_sem, local_sem,
):
    ang_n, row_n, ch_n = sizes
    n = ang_n * row_n * ch_n
    angles, rq, columns = cot_ref.shape
    chans = second_ref.shape[2]
    chans_dev = taps_ref.shape[0]
    held = proj_ref.shape[0]
    both = angles * rq
    half = both // 2
    outer = columns // LANES
    block = outer * half
    rp = masks_ref.shape[2] // (6 * angles)
    team_n = incoming.shape[0]
    team_z, team_k = team_sizes(sizes)
    per = outer // team_n
    slab = lax.axis_index("slab")
    z, k, c0 = lax.axis_index("ang"), lax.axis_index("row"), lax.axis_index("ch")
    me = (z * row_n + k) * ch_n + c0

    def partner(o):
        oz, ok, oc = o // (row_n * ch_n), o // ch_n % row_n, o % ch_n
        return (z + oz) % ang_n, (k + ok) % row_n, (c0 + oc) % ch_n

    def number(at):
        return (at[0] * row_n + at[1]) * ch_n + at[2]

    barrier = pltpu.get_barrier_semaphore()
    loads = [
        pltpu.make_async_copy(source, target, load_sem.at[at])
        for at, (source, target) in enumerate((
            (proj_hbm, proj_ref), (first_hbm, first_vmem), (bias_hbm, bias_vmem),
            (taps_hbm, taps_ref), (cot_hbm, cot_ref), (tables_hbm, tables_ref),
            (turns_hbm, turns_ref), (second_hbm, second_ref),
            (masks_hbm, masks_ref)))
    ]
    loads[0].start()
    each(n, lambda o: pl.semaphore_signal(
        barrier, inc=1, device_id=(slab, *partner(o)), device_id_type=MESH))
    for load in loads[1:]:
        load.start()

    def cols(m):
        return slice(m * LANES, (m + 1) * LANES)

    edge = jnp.zeros((outer, LANES), jnp.float32)
    rows_ref[0:outer, :] = edge
    rows_ref[(held + 1) * outer : (held + 2) * outer, :] = edge
    packed_ref[...] = jnp.zeros(packed_ref.shape, jnp.float32)
    loads[0].wait()
    for at in range(0, held, 8):
        for m in range(outer):
            rows_ref[pl.ds((at + 1) * outer + m, 8, stride=outer), :] = proj_ref[at : at + 8, cols(m)]
    loads[1].wait()
    loads[2].wait()
    for i in range(3):
        packed_ref[:, 3 * i : 3 * i + 3] = first_vmem[i]
    for l in range(chans_dev):
        packed_ref[l : l + 1, 9:10] = bias_vmem[0:1, l : l + 1]
    loads[3].wait()
    pl.semaphore_wait(barrier, n - 1)

    def all_of(source, target, send_sem, recv_sem):
        return pltpu.make_async_remote_copy(
            src_ref=source, dst_ref=target, send_sem=send_sem, recv_sem=recv_sem,
            device_id=(slab, *partner(1)), device_id_type=MESH)

    def rows_copy(o, slot, target):
        start = pl.multiple_of((target * ch_n + c0) * rq * outer, outer)
        return pltpu.make_async_remote_copy(
            src_ref=rows_ref.at[pl.ds(start, (rq + 2) * outer)], dst_ref=got.at[slot, pl.ds(0, (rq + 2) * outer)],
            send_sem=rows_send, recv_sem=rows_recv.at[slot],
            device_id=(slab, target, k, c0), device_id_type=MESH)

    def taps_copy(o, slot, target):
        return pltpu.make_async_remote_copy(
            src_ref=taps_ref, dst_ref=all_taps.at[slot],
            send_sem=taps_send, recv_sem=taps_recv,
            device_id=(slab, z, k, target), device_id_type=MESH)

    def packed_copy(o, slot, target):
        return pltpu.make_async_remote_copy(
            src_ref=packed_ref, dst_ref=all_packed.at[slot],
            send_sem=packed_send, recv_sem=packed_recv,
            device_id=(slab, z, k, target), device_id_type=MESH)

    def top_copy(slot):
        return pltpu.make_async_remote_copy(
            src_ref=rows_ref.at[pl.ds(held * outer, outer)], dst_ref=top.at[slot],
            send_sem=edge_send.at[0], recv_sem=edge_recv.at[0],
            device_id=(slab, 0, (k + 1) % row_n, 0), device_id_type=MESH)

    def bottom_copy(slot):
        return pltpu.make_async_remote_copy(
            src_ref=rows_ref.at[pl.ds(outer, outer)], dst_ref=bottom.at[slot],
            send_sem=edge_send.at[1], recv_sem=edge_recv.at[1],
            device_id=(slab, ang_n - 1, (k + row_n - 1) % row_n, ch_n - 1), device_id_type=MESH)

    for o in range(1, ang_n):
        rows_copy(o, z, (z + o) % ang_n).start()
    for o in range(1, ch_n):
        taps_copy(o, c0, (c0 + o) % ch_n).start()
        packed_copy(o, c0, (c0 + o) % ch_n).start()
    sends_top = jnp.logical_and(c0 == 0, k < row_n - 1)
    sends_bottom = jnp.logical_and(c0 == ch_n - 1, k > 0)

    @pl.when(sends_top)
    def _():
        top_copy(z).start()

    @pl.when(sends_bottom)
    def _():
        bottom_copy(z).start()

    mine_at = pl.multiple_of((z * ch_n + c0) * rq * outer, outer)
    for a in range(ang_n):
        got[a, (rq + 2) * outer : (rq + 3) * outer, :] = jnp.ones((outer, LANES), jnp.float32)
        if rp > rq + 3:
            rest = (rp - rq - 3) * outer
            got[a, (rq + 3) * outer : rp * outer, :] = jnp.zeros((rest, LANES), jnp.float32)
    got[z, 0 : (rq + 2) * outer, :] = rows_ref[pl.ds(mine_at, (rq + 2) * outer), :]
    all_taps[c0] = taps_ref[...]
    all_packed[c0] = packed_ref[...]

    def from_left(x):
        column = lax.broadcasted_iota(jnp.int32, x.shape, 1)
        return jnp.where(column == 0, 0.0, pltpu.roll(x, 1, 1))

    def from_right(x):
        column = lax.broadcasted_iota(jnp.int32, x.shape, 1)
        return jnp.where(column == columns - 1, 0.0, pltpu.roll(x, columns - 1, 1))

    lo, hi = slice(0, half), slice(half, both)
    re_l, im_l = slice(0, LANES), slice(LANES, 2 * LANES)

    loads[4].wait()
    upstream = jnp.concatenate([cot_ref[a] for a in range(angles)], axis=0)
    for i in range(3):
        shift = (i - 1) * rq % both
        turned = pltpu.roll(upstream, shift, 0) if shift else upstream
        cot_shift[3 * i] = from_right(turned)
        cot_shift[3 * i + 1] = turned
        cot_shift[3 * i + 2] = from_left(turned)

    def store_forward(ref, start, values):
        for q, (re, im) in enumerate(short_dft(values, -1)):
            part = slice(q * half, (q + 1) * half)
            cos, sin = turns_ref[0, part, :], turns_ref[1, part, :]
            rows = pl.ds(start + q * half, half)
            ref[rows, re_l] = re * cos + im * sin
            ref[rows, im_l] = im * cos - re * sin

    def load_inverse(ref, start):
        values = []
        for q in range(outer):
            part = slice(q * half, (q + 1) * half)
            cos, sin = turns_ref[0, part, :], turns_ref[1, part, :]
            rows = pl.ds(start + q * half, half)
            re, im = ref[rows, re_l], ref[rows, im_l]
            values.append((re * cos - im * sin, im * cos + re * sin))
        return short_dft(values, 1)

    def start_of(c):
        return pl.multiple_of(c * block, block)

    loads[5].wait()
    loads[6].wait()
    loads[7].wait()

    @pl.loop(0, chans)
    def _(c):
        weights = [second_ref[t // 3, t % 3, c] for t in range(9)]
        values = []
        for m in range(outer):
            pair = []
            for rows in (lo, hi):
                total = weights[0] * cot_shift[0, rows, cols(m)]
                for t in range(1, 9):
                    total = total + weights[t] * cot_shift[t, rows, cols(m)]
                pair.append(total)
            values.append(tuple(pair))
        store_forward(spec_back, start_of(c), values)

    step = 4 * block
    for s in range(0, chans * block, step):
        multiply(spec_back, s, step, tables_ref, 0)

    if ch_n > 1:
        all_of(all_taps.at[pl.ds(0, ch_n - 1)], all_taps.at[pl.ds(0, ch_n - 1)], taps_send, taps_recv).wait_recv()
        all_of(all_packed.at[pl.ds(0, ch_n - 1)], all_packed.at[pl.ds(0, ch_n - 1)], packed_send, packed_recv).wait_recv()
    load_weights = pltpu.make_async_copy(all_packed, first_ref, local_sem)
    load_weights.start()
    taps = jnp.concatenate([all_taps[h] for h in range(ch_n)], axis=0)
    zero = jnp.zeros((chans, LANES), jnp.float32)
    store_forward(spec_taps, 0, [(taps[:, cols(m)], zero) for m in range(outer)])
    multiply(spec_taps, 0, block, tables_ref, 0)

    def tap_row(q, c):
        row = spec_taps[pl.ds(q * half + c, 1), :]
        row = jnp.broadcast_to(row, (half, 2 * LANES))
        return row[:, re_l], row[:, im_l]

    @pl.loop(0, chans)
    def _(c):
        for q in range(outer):
            tr, ti = tap_row(q, c)
            rows = pl.ds(start_of(c) + q * half, half)
            gr, gi = spec_back[rows, re_l], spec_back[rows, im_l]
            work[rows, re_l] = tr * gr - ti * gi
            work[rows, im_l] = tr * gi + ti * gr

    for s in range(0, chans * block, step):
        multiply(work, s, step, tables_ref, 2)

    @pl.loop(0, chans)
    def _(c):
        for m, (re, im) in enumerate(load_inverse(work, start_of(c))):
            back[c, lo, cols(m)] = re
            back[c, hi, cols(m)] = im

    load_weights.wait()
    loads[8].wait()
    for c in range(chans):
        h, l = c // chans_dev, c % chans_dev
        total = first_ref[h, l, 9] * masks_ref[9]
        for t in range(9):
            total = total + first_ref[h, l, t] * masks_ref[t]
        high = total.astype(jnp.bfloat16)
        low = (total - high.astype(jnp.float32)) * masks_ref[10]
        first_matrix[c * both : (c + 1) * both, :] = high
        first_matrix[(chans + c) * both : (chans + c + 1) * both, :] = low.astype(jnp.bfloat16)

    has_top = jnp.logical_and(jnp.logical_and(z == 0, c0 == 0), k > 0)
    has_bottom = jnp.logical_and(jnp.logical_and(z == ang_n - 1, c0 == ch_n - 1), k < row_n - 1)

    @pl.when(has_top)
    def _():
        all_of(top, top, edge_send.at[0], edge_recv.at[0]).wait_recv()

    @pl.when(has_bottom)
    def _():
        all_of(bottom, bottom, edge_send.at[1], edge_recv.at[1]).wait_recv()

    def prepare(a):
        @pl.when(has_top)
        def _():
            got[a, 0:outer, :] = top[a]

        @pl.when(has_bottom)
        def _():
            got[a, (rq + 1) * outer : (rq + 2) * outer, :] = bottom[a]

        centre = jnp.concatenate(
            [got[a, pl.ds(m, rp, stride=outer), :] for m in range(outer)], axis=1)
        lines = jnp.concatenate([from_left(centre), centre, from_right(centre)], axis=0)
        high = lines.astype(jnp.bfloat16).astype(jnp.float32)
        at = pl.multiple_of(a * 6 * rp, 6 * rp)
        lines_ref[pl.ds(at, 6 * rp), :] = jnp.concatenate(
            [high, lines - high], axis=0).astype(jnp.bfloat16)

    prepare(z)
    for o in range(1, ang_n):
        origin = (z + o) % ang_n
        rows_copy(o, origin, origin).wait_recv()
        prepare(origin)

    dot = functools.partial(jnp.dot, preferred_element_type=jnp.float32)
    for at in range(0, columns, 2 * LANES):
        chunk = slice(at, at + 2 * LANES)
        lines = lines_ref[:, chunk]
        total = dot(first_matrix[0 : chans * both, :], lines)
        total = total + dot(first_matrix[chans * both : 2 * chans * both, :], lines)
        gate = 0.5 + 0.5 * jnp.tanh(0.5 * total)
        gate_ref[:, chunk] = gate
        hidden_ref[:, chunk] = total * gate

    @pl.loop(0, chans)
    def _(c):
        at = pl.multiple_of(c * both, both)
        values = []
        for m in range(outer):
            pair = []
            for rows in (pl.ds(at, half), pl.ds(at + half, half)):
                pair.append(hidden_ref[rows, cols(m)])
            values.append(tuple(pair))
        store_forward(spec_hidden, start_of(c), values)

    for s in range(0, chans * block, step):
        multiply(spec_hidden, s, step, tables_ref, 0)

    for q in range(outer):
        rows = [slice(c * block + q * half, c * block + (q + 1) * half) for c in range(chans)]
        at = slice(chans * block + q * half, chans * block + (q + 1) * half)
        reals, imags = [], []
        for line in rows:
            gr, gi = spec_back[line, re_l], spec_back[line, im_l]
            hr, hi_ = spec_hidden[line, re_l], spec_hidden[line, im_l]
            reals.append(gr * hr + gi * hi_)
            imags.append(gr * hi_ - gi * hr)
        work[at, re_l] = fold_rows(reals)
        work[at, im_l] = fold_rows(imags)

    multiply(work, chans * block, block, tables_ref, 2)
    for m, (re, im) in enumerate(load_inverse(work, chans * block)):
        outgoing[m] = re

    def folded(value):
        return jnp.sum(value, axis=0, keepdims=True)

    def mate(o):
        oz, ok, oc = o // (team_k * ch_n), o // ch_n % team_k, o % ch_n
        there_z = z // team_z * team_z + (z + oz) % team_z
        there_k = k // team_k * team_k + (k + ok) % team_k
        return there_z, there_k, (c0 + oc) % ch_n

    def rank(at):
        return (at[0] % team_z * team_k + at[1] % team_k) * ch_n + at[2]

    def sum_copy(o):
        target = mate(o)
        return pltpu.make_async_remote_copy(
            src_ref=outgoing.at[pl.ds(rank(target) * per, per)], dst_ref=incoming.at[o],
            send_sem=sum_send, recv_sem=sum_recv,
            device_id=(slab, *target), device_id_type=MESH)

    each(team_n, lambda o: sum_copy(o).start())

    for a in range(angles):
        for i in range(3):
            for m in range(outer):
                lines = got[a, pl.ds(i * outer + m, rq, stride=outer), :]
                proj_shift[3 * i + 1, a * rq : (a + 1) * rq, cols(m)] = lines
    for i in range(3):
        centre = proj_shift[3 * i + 1]
        proj_shift[3 * i] = from_left(centre)
        proj_shift[3 * i + 2] = from_right(centre)

    @pl.loop(0, chans)
    def _(c):
        for q in range(outer):
            tr, ti = tap_row(q, c)
            rows = pl.ds(start_of(c) + q * half, half)
            hr, hi_ = spec_hidden[rows, re_l], spec_hidden[rows, im_l]
            work[rows, re_l] = tr * hr + ti * hi_
            work[rows, im_l] = tr * hi_ - ti * hr

    for s in range(0, chans * block, step):
        multiply(work, s, step, tables_ref, 2)

    partial[...] = jnp.zeros(partial.shape, jnp.float32)

    @pl.loop(0, chans)
    def _(c):
        sums = [jnp.zeros((half, LANES), jnp.float32) for _ in range(10)]
        for m in range(outer):
            for rows in (lo, hi):
                at = pl.ds(pl.multiple_of(c * both, both) + rows.start, half)
                gate = gate_ref[at, cols(m)]
                slope = gate + hidden_ref[at, cols(m)] * (1.0 - gate)
                grad = back[c, rows, cols(m)] * slope
                for t in range(9):
                    sums[t] = sums[t] + grad * proj_shift[t, rows, cols(m)]
                sums[9] = sums[9] + grad
        for t in range(10):
            partial[c, t : t + 1, :] = folded(sums[t])

    @pl.loop(0, chans)
    def _(c):
        sums = [jnp.zeros((half, LANES), jnp.float32) for _ in range(9)]
        for m, (re, im) in enumerate(load_inverse(work, start_of(c))):
            filt[c, lo, cols(m)] = re
            filt[c, hi, cols(m)] = im
            for t in range(9):
                sums[t] = sums[t] + re * cot_shift[t, lo, cols(m)] + im * cot_shift[t, hi, cols(m)]
        for t in range(9):
            partial[c, 16 + t : 17 + t, :] = folded(sums[t])

    small = lax.dot_general(
        jnp.ones((8, LANES), jnp.float32), partial[...].reshape(chans * SLOTS, LANES),
        (((1,), (1,)), ((), ())),
        precision=lax.Precision.HIGHEST, preferred_element_type=jnp.float32)
    width = chans_dev * SLOTS
    for h in range(ch_n):
        small_own[h] = small[0:1, h * width : (h + 1) * width]

    mine = pl.multiple_of(rank((z, k, c0)) * per, per)
    total = outgoing[pl.ds(mine, per)]
    summed = incoming.at[pl.ds(1, team_n - 1)]
    all_of(summed, summed, sum_send, sum_recv).wait_recv()
    for o in range(1, team_n):
        total = total + incoming[o]
    used = per * chans_dev
    for h in range(ch_n):
        for p in range(per):
            at = slice(p * chans_dev, (p + 1) * chans_dev)
            spread[h, at, :] = total[p, h * chans_dev : (h + 1) * chans_dev]
        spread[h, used : used + 1, :] = small_own[h]
    spreads = gathered.at[pl.ds(0, n - 1), pl.ds(0, used + 1)]

    def gather_copy(o):
        target = partner(o)
        return pltpu.make_async_remote_copy(
            src_ref=spread.at[target[2], pl.ds(0, used + 1)], dst_ref=gathered.at[me, pl.ds(0, used + 1)],
            send_sem=gather_send, recv_sem=gather_recv,
            device_id=(slab, *target), device_id_type=MESH)

    each(n, lambda o: gather_copy(o).start())
    gathered[me] = spread[c0]

    @pl.loop(0, outer)
    def _(m):
        at = pl.ds(pl.multiple_of(m * LANES, LANES), LANES)
        for rows in (lo, hi):
            pieces = [filt[c, rows, at] for c in range(chans)]
            for t in range(9):
                total = second_ref[t // 3, t % 3, 0] * pieces[0]
                for c in range(1, chans):
                    total = total + second_ref[t // 3, t % 3, c] * pieces[c]
                mixed[t, rows, at] = total

    sides = []
    for j in range(3):
        total = mixed[3 + j]
        for i in (0, 2):
            total = total + pltpu.roll(mixed[3 * i + j], -(i - 1) * rq % both, 0)
        sides.append(total)
    image = sides[1] + from_left(sides[0]) + from_right(sides[2])
    for a in range(angles):
        sino_ref[a] = image[a * rq : (a + 1) * rq]

    all_of(spreads, spreads, gather_send, gather_recv).wait_recv()
    sums = gathered[0, used : used + 1, :]
    for d in range(1, n):
        sums = sums + gathered[d, used : used + 1, :]
    for l in range(chans_dev):
        for i in range(3):
            at = l * SLOTS + 3 * i
            first_out_ref[i, l : l + 1, :] = sums[:, at : at + 3]
            second_out_ref[i, l : l + 1, :] = sums[:, at + 16 : at + 19]
        bias_out_ref[0:1, l : l + 1] = sums[:, l * SLOTS + 9 : l * SLOTS + 10]

    for m in range(outer):
        owner, at = m // per, m % per
        rz, rk, rc = owner // (team_k * ch_n), owner // ch_n % team_k, owner % ch_n
        pieces = [
            gathered[number((jz + rz, jk + rk, rc)), at * chans_dev : (at + 1) * chans_dev, :]
            for jz in range(0, ang_n, team_z) for jk in range(0, row_n, team_k)]
        taps_out_ref[:, cols(m)] = functools.reduce(lambda x, y: x + y, pieces)

    if ang_n > 1:
        sent = got.at[pl.ds(0, ang_n - 1), pl.ds(0, (rq + 2) * outer)]
        all_of(sent, sent, rows_send, rows_recv.at[0]).wait_send()
    if ch_n > 1:
        sent = all_taps.at[pl.ds(0, ch_n - 1)]
        all_of(sent, sent, taps_send, taps_recv).wait_send()
        sent = all_packed.at[pl.ds(0, ch_n - 1)]
        all_of(sent, sent, packed_send, packed_recv).wait_send()

    @pl.when(sends_top)
    def _():
        top_copy(z).wait_send()

    @pl.when(sends_bottom)
    def _():
        bottom_copy(z).wait_send()

    all_of(summed, summed, sum_send, sum_recv).wait_send()
    all_of(spreads, spreads, gather_send, gather_recv).wait_send()


def deliver(*refs):
    count = (len(refs) - 1) // 2
    sources, targets, sems = refs[:count], refs[count : 2 * count], refs[-1]
    copies = [pltpu.make_async_copy(sources[at], targets[at], sems.at[at]) for at in range(count)]
    for copy in copies:
        copy.start()
    for copy in copies:
        copy.wait()


def on_device(sizes, tables, projections, conv1_weight, conv1_bias, filter_taps, conv2_weight, cotangent):
    ang_n, row_n, ch_n = sizes
    n = ang_n * row_n * ch_n
    _, held, columns = projections.shape
    chans_dev = conv1_weight.shape[0]
    chans = chans_dev * ch_n
    _, angles, rq, _ = cotangent.shape
    outer = columns // LANES
    both = angles * rq
    block = outer * both // 2
    rp = padded_rows(rq)
    team_n = math.prod(team_sizes(sizes)) * ch_n
    slot = -(-(outer // team_n * chans_dev + 1) // 8) * 8
    f32 = jnp.float32
    vmem = pl.BlockSpec(memory_space=pltpu.VMEM)
    hbm = pl.BlockSpec(memory_space=pltpu.HBM)
    dma = pltpu.SemaphoreType.DMA
    wide = (both, columns)
    shapes = (
        jax.ShapeDtypeStruct((angles, rq, columns), f32),
        jax.ShapeDtypeStruct((3, chans_dev, 3), f32),
        jax.ShapeDtypeStruct((1, chans_dev), f32),
        jax.ShapeDtypeStruct((chans_dev, columns), f32),
        jax.ShapeDtypeStruct((3, chans_dev, 3), f32),
    )
    results = pl.pallas_call(
        functools.partial(kernel, sizes),
        out_shape=tuple(pltpu.VMEM(leaf.shape, f32) for leaf in shapes),
        in_specs=[hbm] * 9,
        out_specs=(vmem,) * 5,
        scratch_shapes=[
            pltpu.VMEM((held, columns), f32),
            pltpu.VMEM((3, chans_dev, 3), f32),
            pltpu.VMEM((1, chans_dev), f32),
            pltpu.VMEM((chans_dev, columns), f32),
            pltpu.VMEM((angles, rq, columns), f32),
            pltpu.VMEM(tables[0].shape, jnp.bfloat16),
            pltpu.VMEM(tables[1].shape, f32),
            pltpu.VMEM(tables[2].shape, f32),
            pltpu.VMEM(((held + 2) * outer, LANES), f32),
            pltpu.VMEM((chans_dev, LANES), f32),
            pltpu.VMEM((ch_n, 1, LANES), f32),
            pltpu.VMEM((ang_n, rp * outer, LANES), f32),
            pltpu.VMEM((ang_n, outer, LANES), f32),
            pltpu.VMEM((ang_n, outer, LANES), f32),
            pltpu.VMEM((ch_n, chans_dev, columns), f32),
            pltpu.VMEM((ch_n, chans_dev, LANES), f32),
            pltpu.SMEM((ch_n, chans_dev, LANES), f32),
            pltpu.SMEM((3, 3, chans), f32),
            pltpu.VMEM((9,) + wide, f32),
            pltpu.VMEM((9,) + wide, f32),
            pltpu.VMEM((chans * block, 2 * LANES), f32),
            pltpu.VMEM((chans * block, 2 * LANES), f32),
            pltpu.VMEM((block, 2 * LANES), f32),
            pltpu.VMEM(((chans + 1) * block, 2 * LANES), f32),
            pltpu.VMEM((chans,) + wide, f32),
            pltpu.VMEM((chans * both, columns), f32),
            pltpu.VMEM((chans * both, columns), f32),
            pltpu.VMEM((chans,) + wide, f32),
            pltpu.VMEM((chans, SLOTS, LANES), f32),
            pltpu.VMEM((9,) + wide, f32),
            pltpu.VMEM((angles * 6 * rp, columns), jnp.bfloat16),
            pltpu.VMEM((2 * chans * both, angles * 6 * rp), jnp.bfloat16),
            pltpu.VMEM((outer, chans, LANES), f32),
            pltpu.VMEM((team_n, outer // team_n, chans, LANES), f32),
            pltpu.VMEM((ch_n, slot, LANES), f32),
            pltpu.VMEM((n, slot, LANES), f32),
            dma(()), dma((ang_n,)), dma((2,)), dma((2,)),
            dma(()), dma(()), dma(()), dma(()),
            dma(()), dma(()), dma(()), dma(()), dma((9,)), dma(()),
        ],
        compiler_params=pltpu.CompilerParams(
            collective_id=0, has_side_effects=True, vmem_limit_bytes=63 * 2**20
        ),
        name="tomography",
    )(
        projections[0], jnp.transpose(conv1_weight, (1, 0, 2)), conv1_bias[None], filter_taps,
        jnp.transpose(conv2_weight, (1, 2, 0)), cotangent[0], *tables,
    )
    image, first, bias, taps_out, second = pl.pallas_call(
        deliver,
        out_shape=shapes,
        in_specs=[vmem] * 5,
        out_specs=(hbm,) * 5,
        scratch_shapes=[dma((5,))],
        name="deliver",
    )(*[pltpu.with_memory_space_constraint(leaf, pltpu.VMEM) for leaf in results])
    return (
        image[None], jnp.transpose(first, (1, 0, 2)), bias[0], taps_out,
        jnp.transpose(second, (1, 0, 2)),
    )


def solution(mesh):
    sizes = tuple(mesh.shape[axis] for axis in ("ang", "row", "ch"))

    def whole(projections, conv1_weight, conv1_bias, filter_taps, conv2_weight, cotangent):
        angles, rq = cotangent.shape[1], cotangent.shape[2] // (sizes[0] * sizes[2])
        tables = (*make_tables(projections.shape[-1]), make_masks(angles, rq))

        def local(*arrays):
            return on_device(sizes, tuple(jnp.asarray(t) for t in tables), *arrays)

        return jax.shard_map(
            local,
            mesh=mesh,
            in_specs=(
                P(("slab", "ang"), "row", None),
                P("ch", None, None),
                P("ch"),
                P("ch", None),
                P(),
                P(("slab", "row"), None, ("ang", "ch"), None),
            ),
            out_specs=(
                P(("slab", "row"), None, ("ang", "ch"), None),
                P(("slab", "ch"), None, None),
                P(("slab", "ch")),
                P(("slab", "ch"), None),
                P(("slab", "ch"), None, None),
            ),
            check_vma=False,
        )(projections, conv1_weight, conv1_bias, filter_taps, conv2_weight, cotangent)

    return whole
```

```python
import functools
import math

import jax
import jax.numpy as jnp
import numpy as np
import ml_dtypes
from jax import lax
from jax.experimental import pallas as pl
from jax.experimental.pallas import tpu as pltpu
from jax.sharding import PartitionSpec as P

MESH = pl.DeviceIdType.MESH
LANES = 128
SLOTS = 32


def twisted(value, k, n, sign):
    re, im = value
    if k == 0:
        return value
    if 4 * k == n:
        return (-im, re) if sign > 0 else (im, -re)
    if 8 * k == n:
        half = math.sqrt(0.5)
        return (half * (re - sign * im), half * (im + sign * re))
    if 8 * k == 3 * n:
        half = math.sqrt(0.5)
        return (half * (-re - sign * im), half * (-im + sign * re))
    cos = math.cos(2 * math.pi * k / n)
    sin = sign * math.sin(2 * math.pi * k / n)
    return (cos * re - sin * im, cos * im + sin * re)


def short_dft(values, sign):
    n = len(values)
    if n == 1:
        return values
    even = short_dft(values[0::2], sign)
    odd = short_dft(values[1::2], sign)
    low, high = [], []
    for k in range(n // 2):
        re, im = twisted(odd[k], k, n, sign)
        low.append((even[k][0] + re, even[k][1] + im))
        high.append((even[k][0] - re, even[k][1] - im))
    return low + high


def split_high_low(table):
    high = table.astype(ml_dtypes.bfloat16)
    low = (table - high.astype(np.float64)).astype(ml_dtypes.bfloat16)
    return high, low


def make_tables(length):
    outer = length // LANES
    index = np.arange(LANES)
    inner = 2 * np.pi * (np.outer(index, index) % LANES) / LANES
    cos, sin = np.cos(inner), np.sin(inner)
    forward = np.block([[cos, -sin], [sin, cos]])
    inverse = np.block([[cos, sin], [-sin, cos]]) / length
    twist = 2 * np.pi * np.outer(np.arange(outer), index) / length
    twist = np.repeat(twist, 8, axis=0)
    tables = np.stack([*split_high_low(forward), *split_high_low(inverse)])
    turns = np.stack([np.cos(twist), np.sin(twist)]).astype(np.float32)
    return tables, turns


def padded_rows(rq):
    return -(-(rq + 3) // 8) * 8


def make_masks(angles, rq):
    rp = padded_rows(rq)
    masks = np.zeros((11, angles, rq, angles, 2, 3, rp), np.float32)
    for a in range(angles):
        for r in range(rq):
            for t in range(9):
                masks[t, a, r, a, :, t % 3, r + t // 3] = 1
            masks[9, a, r, a, 0, 1, rq + 2] = 1
            masks[10, a, r, :, 0] = 1
    masks = masks.reshape(11, angles * rq, angles * 6 * rp)
    return np.pad(masks, ((0, 0), (0, 0), (0, -masks.shape[2] % LANES)))


def fold_rows(values):
    count = len(values)
    line = lax.broadcasted_iota(jnp.int32, values[0].shape, 0)
    step = count // 2
    while step:
        first = (line & step) == 0
        values = [
            jnp.where(first, a, b)
            + jnp.where(first, pltpu.roll(a, count - step, 0), pltpu.roll(b, step, 0))
            for a, b in zip(values[:step], values[step:])
        ]
        step //= 2
    return values[0]


def multiply(ref, start, rows, tables_ref, which):
    values = ref[pl.ds(start, rows), :]
    high = values.astype(jnp.bfloat16)
    low = (values - high.astype(jnp.float32)).astype(jnp.bfloat16)
    dot = functools.partial(jnp.dot, preferred_element_type=jnp.float32)
    table_high = tables_ref[which]
    ref[pl.ds(start, rows), :] = (
        dot(high, table_high) + dot(low, table_high) + dot(high, tables_ref[which + 1])
    )


def team_sizes(sizes):
    return tuple(2 if size % 2 == 0 else 1 for size in sizes[:2])


def each(count, body):
    if count <= 32:
        for o in range(1, count):
            body(o)
    else:
        pl.loop(1, count)(body)


def kernel(
    sizes,
    proj_hbm, first_hbm, bias_hbm, taps_hbm, second_hbm, cot_hbm, tables_hbm, turns_hbm, masks_hbm,
    sino_ref, first_out_ref, bias_out_ref, taps_out_ref, second_out_ref,
    proj_ref, first_vmem, bias_vmem, taps_ref, cot_ref, tables_ref, turns_ref, masks_ref,
    rows_ref, packed_ref, small_own,
    got, top, bottom, all_taps, all_packed, first_ref, second_ref,
    cot_shift, spec_back, spec_hidden, spec_taps, work,
    back, hidden_ref, gate_ref, filt, partial, mixed, lines_ref, first_matrix, grads_ref,
    outgoing, incoming, spread, gathered,
    rows_send, rows_recv, edge_send, edge_recv, taps_send, taps_recv,
    packed_send, packed_recv, sum_send, sum_recv, gather_send, gather_recv, load_sem, local_sem,
):
    ang_n, row_n, ch_n = sizes
    n = ang_n * row_n * ch_n
    angles, rq, columns = cot_ref.shape
    chans = second_ref.shape[2]
    chans_dev = taps_ref.shape[0]
    held = proj_ref.shape[0]
    both = angles * rq
    half = both // 2
    outer = columns // LANES
    block = outer * half
    depth = lines_ref.shape[0]
    rp = depth // (6 * angles)
    team_n = incoming.shape[0]
    team_z, team_k = team_sizes(sizes)
    per = outer // team_n
    slab = lax.axis_index("slab")
    z, k, c0 = lax.axis_index("ang"), lax.axis_index("row"), lax.axis_index("ch")
    me = (z * row_n + k) * ch_n + c0

    def partner(o):
        oz, ok, oc = o // (row_n * ch_n), o // ch_n % row_n, o % ch_n
        return (z + oz) % ang_n, (k + ok) % row_n, (c0 + oc) % ch_n

    def number(at):
        return (at[0] * row_n + at[1]) * ch_n + at[2]

    barrier = pltpu.get_barrier_semaphore()
    loads = [
        pltpu.make_async_copy(source, target, load_sem.at[at])
        for at, (source, target) in enumerate((
            (proj_hbm, proj_ref), (first_hbm, first_vmem), (bias_hbm, bias_vmem),
            (taps_hbm, taps_ref), (cot_hbm, cot_ref), (tables_hbm, tables_ref),
            (turns_hbm, turns_ref), (second_hbm, second_ref),
            (masks_hbm, masks_ref)))
    ]
    loads[0].start()
    each(n, lambda o: pl.semaphore_signal(
        barrier, inc=1, device_id=(slab, *partner(o)), device_id_type=MESH))
    for load in loads[1:]:
        load.start()

    def cols(m):
        return slice(m * LANES, (m + 1) * LANES)

    edge = jnp.zeros((outer, LANES), jnp.float32)
    rows_ref[0:outer, :] = edge
    rows_ref[(held + 1) * outer : (held + 2) * outer, :] = edge
    packed_ref[...] = jnp.zeros(packed_ref.shape, jnp.float32)
    loads[0].wait()
    for at in range(0, held, 8):
        for m in range(outer):
            rows_ref[pl.ds((at + 1) * outer + m, 8, stride=outer), :] = proj_ref[at : at + 8, cols(m)]
    loads[1].wait()
    loads[2].wait()
    for i in range(3):
        packed_ref[:, 3 * i : 3 * i + 3] = first_vmem[i]
    for l in range(chans_dev):
        packed_ref[l : l + 1, 9:10] = bias_vmem[0:1, l : l + 1]
    loads[3].wait()
    pl.semaphore_wait(barrier, n - 1)

    def all_of(source, target, send_sem, recv_sem):
        return pltpu.make_async_remote_copy(
            src_ref=source, dst_ref=target, send_sem=send_sem, recv_sem=recv_sem,
            device_id=(slab, *partner(1)), device_id_type=MESH)

    def rows_copy(o, slot, target):
        start = pl.multiple_of((target * ch_n + c0) * rq * outer, outer)
        return pltpu.make_async_remote_copy(
            src_ref=rows_ref.at[pl.ds(start, (rq + 2) * outer)], dst_ref=got.at[slot, pl.ds(0, (rq + 2) * outer)],
            send_sem=rows_send, recv_sem=rows_recv.at[slot],
            device_id=(slab, target, k, c0), device_id_type=MESH)

    def taps_copy(o, slot, target):
        return pltpu.make_async_remote_copy(
            src_ref=taps_ref, dst_ref=all_taps.at[slot],
            send_sem=taps_send, recv_sem=taps_recv,
            device_id=(slab, z, k, target), device_id_type=MESH)

    def packed_copy(o, slot, target):
        return pltpu.make_async_remote_copy(
            src_ref=packed_ref, dst_ref=all_packed.at[slot],
            send_sem=packed_send, recv_sem=packed_recv,
            device_id=(slab, z, k, target), device_id_type=MESH)

    def top_copy(slot):
        return pltpu.make_async_remote_copy(
            src_ref=rows_ref.at[pl.ds(held * outer, outer)], dst_ref=top.at[slot],
            send_sem=edge_send.at[0], recv_sem=edge_recv.at[0],
            device_id=(slab, 0, (k + 1) % row_n, 0), device_id_type=MESH)

    def bottom_copy(slot):
        return pltpu.make_async_remote_copy(
            src_ref=rows_ref.at[pl.ds(outer, outer)], dst_ref=bottom.at[slot],
            send_sem=edge_send.at[1], recv_sem=edge_recv.at[1],
            device_id=(slab, ang_n - 1, (k + row_n - 1) % row_n, ch_n - 1), device_id_type=MESH)

    for o in range(1, ang_n):
        rows_copy(o, z, (z + o) % ang_n).start()
    for o in range(1, ch_n):
        taps_copy(o, c0, (c0 + o) % ch_n).start()
        packed_copy(o, c0, (c0 + o) % ch_n).start()
    sends_top = jnp.logical_and(c0 == 0, k < row_n - 1)
    sends_bottom = jnp.logical_and(c0 == ch_n - 1, k > 0)

    @pl.when(sends_top)
    def _():
        top_copy(z).start()

    @pl.when(sends_bottom)
    def _():
        bottom_copy(z).start()

    mine_at = pl.multiple_of((z * ch_n + c0) * rq * outer, outer)
    for a in range(ang_n):
        got[a, (rq + 2) * outer : (rq + 3) * outer, :] = jnp.ones((outer, LANES), jnp.float32)
        if rp > rq + 3:
            rest = (rp - rq - 3) * outer
            got[a, (rq + 3) * outer : rp * outer, :] = jnp.zeros((rest, LANES), jnp.float32)
    got[z, 0 : (rq + 2) * outer, :] = rows_ref[pl.ds(mine_at, (rq + 2) * outer), :]
    all_taps[c0] = taps_ref[...]
    all_packed[c0] = packed_ref[...]

    def from_left(x):
        column = lax.broadcasted_iota(jnp.int32, x.shape, 1)
        return jnp.where(column == 0, 0.0, pltpu.roll(x, 1, 1))

    def from_right(x):
        column = lax.broadcasted_iota(jnp.int32, x.shape, 1)
        return jnp.where(column == columns - 1, 0.0, pltpu.roll(x, columns - 1, 1))

    lo, hi = slice(0, half), slice(half, both)
    re_l, im_l = slice(0, LANES), slice(LANES, 2 * LANES)

    loads[4].wait()
    upstream = jnp.concatenate([cot_ref[a] for a in range(angles)], axis=0)
    for i in range(3):
        shift = (i - 1) * rq % both
        turned = pltpu.roll(upstream, shift, 0) if shift else upstream
        cot_shift[3 * i] = from_right(turned)
        cot_shift[3 * i + 1] = turned
        cot_shift[3 * i + 2] = from_left(turned)

    def store_forward(ref, start, values):
        for q, (re, im) in enumerate(short_dft(values, -1)):
            part = slice(q * half, (q + 1) * half)
            cos, sin = turns_ref[0, part, :], turns_ref[1, part, :]
            rows = pl.ds(start + q * half, half)
            ref[rows, re_l] = re * cos + im * sin
            ref[rows, im_l] = im * cos - re * sin

    def load_inverse(ref, start):
        values = []
        for q in range(outer):
            part = slice(q * half, (q + 1) * half)
            cos, sin = turns_ref[0, part, :], turns_ref[1, part, :]
            rows = pl.ds(start + q * half, half)
            re, im = ref[rows, re_l], ref[rows, im_l]
            values.append((re * cos - im * sin, im * cos + re * sin))
        return short_dft(values, 1)

    def start_of(c):
        return pl.multiple_of(c * block, block)

    loads[5].wait()
    loads[6].wait()
    loads[7].wait()

    @pl.loop(0, chans)
    def _(c):
        weights = [second_ref[t // 3, t % 3, c] for t in range(9)]
        values = []
        for m in range(outer):
            pair = []
            for rows in (lo, hi):
                total = weights[0] * cot_shift[0, rows, cols(m)]
                for t in range(1, 9):
                    total = total + weights[t] * cot_shift[t, rows, cols(m)]
                pair.append(total)
            values.append(tuple(pair))
        store_forward(spec_back, start_of(c), values)

    step = 4 * block
    for s in range(0, chans * block, step):
        multiply(spec_back, s, step, tables_ref, 0)

    if ch_n > 1:
        all_of(all_taps.at[pl.ds(0, ch_n - 1)], all_taps.at[pl.ds(0, ch_n - 1)], taps_send, taps_recv).wait_recv()
        all_of(all_packed.at[pl.ds(0, ch_n - 1)], all_packed.at[pl.ds(0, ch_n - 1)], packed_send, packed_recv).wait_recv()
    load_weights = pltpu.make_async_copy(all_packed, first_ref, local_sem)
    load_weights.start()
    taps = jnp.concatenate([all_taps[h] for h in range(ch_n)], axis=0)
    zero = jnp.zeros((chans, LANES), jnp.float32)
    store_forward(spec_taps, 0, [(taps[:, cols(m)], zero) for m in range(outer)])
    multiply(spec_taps, 0, block, tables_ref, 0)

    def tap_row(q, c):
        row = spec_taps[pl.ds(q * half + c, 1), :]
        row = jnp.broadcast_to(row, (half, 2 * LANES))
        return row[:, re_l], row[:, im_l]

    @pl.loop(0, chans)
    def _(c):
        for q in range(outer):
            tr, ti = tap_row(q, c)
            rows = pl.ds(start_of(c) + q * half, half)
            gr, gi = spec_back[rows, re_l], spec_back[rows, im_l]
            work[rows, re_l] = tr * gr - ti * gi
            work[rows, im_l] = tr * gi + ti * gr

    for s in range(0, chans * block, step):
        multiply(work, s, step, tables_ref, 2)

    @pl.loop(0, chans)
    def _(c):
        for m, (re, im) in enumerate(load_inverse(work, start_of(c))):
            back[c, lo, cols(m)] = re
            back[c, hi, cols(m)] = im

    load_weights.wait()
    loads[8].wait()
    for c in range(chans):
        h, l = c // chans_dev, c % chans_dev
        total = first_ref[h, l, 9] * masks_ref[9]
        for t in range(9):
            total = total + first_ref[h, l, t] * masks_ref[t]
        high = total.astype(jnp.bfloat16)
        low = (total - high.astype(jnp.float32)) * masks_ref[10]
        first_matrix[c * both : (c + 1) * both, :] = high[:, 0:depth]
        first_matrix[(chans + c) * both : (chans + c + 1) * both, :] = low[:, 0:depth].astype(jnp.bfloat16)

    has_top = jnp.logical_and(jnp.logical_and(z == 0, c0 == 0), k > 0)
    has_bottom = jnp.logical_and(jnp.logical_and(z == ang_n - 1, c0 == ch_n - 1), k < row_n - 1)

    @pl.when(has_top)
    def _():
        all_of(top, top, edge_send.at[0], edge_recv.at[0]).wait_recv()

    @pl.when(has_bottom)
    def _():
        all_of(bottom, bottom, edge_send.at[1], edge_recv.at[1]).wait_recv()

    def prepare(a):
        @pl.when(has_top)
        def _():
            got[a, 0:outer, :] = top[a]

        @pl.when(has_bottom)
        def _():
            got[a, (rq + 1) * outer : (rq + 2) * outer, :] = bottom[a]

        centre = jnp.concatenate(
            [got[a, pl.ds(m, rp, stride=outer), :] for m in range(outer)], axis=1)
        lines = jnp.concatenate([from_left(centre), centre, from_right(centre)], axis=0)
        high = lines.astype(jnp.bfloat16).astype(jnp.float32)
        at = pl.multiple_of(a * 6 * rp, 6 * rp)
        lines_ref[pl.ds(at, 6 * rp), :] = jnp.concatenate(
            [high, lines - high], axis=0).astype(jnp.bfloat16)

    prepare(z)
    for o in range(1, ang_n):
        origin = (z + o) % ang_n
        rows_copy(o, origin, origin).wait_recv()
        prepare(origin)

    dot = functools.partial(jnp.dot, preferred_element_type=jnp.float32)
    for at in range(0, columns, 2 * LANES):
        chunk = slice(at, at + 2 * LANES)
        lines = lines_ref[:, chunk]
        total = dot(first_matrix[...], lines)
        total = total[0 : chans * both] + total[chans * both : 2 * chans * both]
        gate = 0.5 + 0.5 * jnp.tanh(0.5 * total)
        gate_ref[:, chunk] = gate
        hidden_ref[:, chunk] = total * gate

    for c in range(chans):
        values = []
        for m in range(outer):
            values.append(tuple(
                hidden_ref[at : at + half, cols(m)] for at in (c * both, c * both + half)))
        store_forward(spec_hidden, c * block, values)
        if (c + 1) % 4 == 0:
            multiply(spec_hidden, (c + 1 - 4) * block, 4 * block, tables_ref, 0)

    for q in range(outer):
        rows = [slice(c * block + q * half, c * block + (q + 1) * half) for c in range(chans)]
        at = slice(chans * block + q * half, chans * block + (q + 1) * half)
        reals, imags = [], []
        for line in rows:
            gr, gi = spec_back[line, re_l], spec_back[line, im_l]
            hr, hi_ = spec_hidden[line, re_l], spec_hidden[line, im_l]
            reals.append(gr * hr + gi * hi_)
            imags.append(gr * hi_ - gi * hr)
        work[at, re_l] = fold_rows(reals)
        work[at, im_l] = fold_rows(imags)

    multiply(work, chans * block, block, tables_ref, 2)
    for m, (re, im) in enumerate(load_inverse(work, chans * block)):
        outgoing[m] = re

    def folded(value):
        return jnp.sum(value, axis=0, keepdims=True)

    def mate(o):
        oz, ok, oc = o // (team_k * ch_n), o // ch_n % team_k, o % ch_n
        there_z = z // team_z * team_z + (z + oz) % team_z
        there_k = k // team_k * team_k + (k + ok) % team_k
        return there_z, there_k, (c0 + oc) % ch_n

    def rank(at):
        return (at[0] % team_z * team_k + at[1] % team_k) * ch_n + at[2]

    def sum_copy(o):
        target = mate(o)
        return pltpu.make_async_remote_copy(
            src_ref=outgoing.at[pl.ds(rank(target) * per, per)], dst_ref=incoming.at[o],
            send_sem=sum_send, recv_sem=sum_recv,
            device_id=(slab, *target), device_id_type=MESH)

    each(team_n, lambda o: sum_copy(o).start())

    @pl.loop(0, chans)
    def _(c):
        for q in range(outer):
            tr, ti = tap_row(q, c)
            rows = pl.ds(start_of(c) + q * half, half)
            hr, hi_ = spec_hidden[rows, re_l], spec_hidden[rows, im_l]
            work[rows, re_l] = tr * hr + ti * hi_
            work[rows, im_l] = tr * hi_ - ti * hr

    for s in range(0, chans * block, step):
        multiply(work, s, step, tables_ref, 2)

    partial[...] = jnp.zeros(partial.shape, jnp.float32)

    @pl.loop(0, chans)
    def _(c):
        at = pl.ds(pl.multiple_of(c * both, both), both)
        at_low = pl.ds(pl.multiple_of((chans + c) * both, both), both)
        for m in range(outer):
            gate = gate_ref[at, cols(m)]
            grad = back[c, :, cols(m)] * (gate + hidden_ref[at, cols(m)] * (1.0 - gate))
            high = grad.astype(jnp.bfloat16)
            grads_ref[at, cols(m)] = high
            grads_ref[at_low, cols(m)] = (grad - high.astype(jnp.float32)).astype(jnp.bfloat16)

    total = lax.dot_general(
        grads_ref[...], lines_ref[...], (((1,), (1,)), ((), ())),
        preferred_element_type=jnp.float32)
    total = total[0 : chans * both] + total[chans * both : 2 * chans * both]
    wide = masks_ref.shape[2]
    if wide > depth:
        total = jnp.concatenate([total, jnp.zeros((chans * both, wide - depth), jnp.float32)], axis=1)
    for c in range(chans):
        values = []
        for t in range(10):
            value = total[c * both : (c + 1) * both] * masks_ref[t]
            value = value[0:half] + value[half:both]
            values.append(functools.reduce(
                lambda x, y: x + y, [value[:, at : at + LANES] for at in range(0, wide, LANES)]))
        partial[c, 0:8, :] = fold_rows(values[0:8])
        partial[c, 8:9, :] = folded(values[8])
        partial[c, 9:10, :] = folded(values[9])

    @pl.loop(0, chans)
    def _(c):
        sums = [jnp.zeros((half, LANES), jnp.float32) for _ in range(9)]
        for m, (re, im) in enumerate(load_inverse(work, start_of(c))):
            filt[c, lo, cols(m)] = re
            filt[c, hi, cols(m)] = im
            for t in range(9):
                sums[t] = sums[t] + re * cot_shift[t, lo, cols(m)] + im * cot_shift[t, hi, cols(m)]
        for t in range(9):
            partial[c, 16 + t : 17 + t, :] = folded(sums[t])

    small = lax.dot_general(
        jnp.ones((8, LANES), jnp.float32), partial[...].reshape(chans * SLOTS, LANES),
        (((1,), (1,)), ((), ())),
        precision=lax.Precision.HIGHEST, preferred_element_type=jnp.float32)
    width = chans_dev * SLOTS
    for h in range(ch_n):
        small_own[h] = small[0:1, h * width : (h + 1) * width]

    mine = pl.multiple_of(rank((z, k, c0)) * per, per)
    total = outgoing[pl.ds(mine, per)]
    summed = incoming.at[pl.ds(1, team_n - 1)]
    all_of(summed, summed, sum_send, sum_recv).wait_recv()
    for o in range(1, team_n):
        total = total + incoming[o]
    used = per * chans_dev
    for h in range(ch_n):
        for p in range(per):
            at = slice(p * chans_dev, (p + 1) * chans_dev)
            spread[h, at, :] = total[p, h * chans_dev : (h + 1) * chans_dev]
        spread[h, used : used + 1, :] = small_own[h]
    spreads = gathered.at[pl.ds(0, n - 1), pl.ds(0, used + 1)]

    def gather_copy(o):
        target = partner(o)
        return pltpu.make_async_remote_copy(
            src_ref=spread.at[target[2], pl.ds(0, used + 1)], dst_ref=gathered.at[me, pl.ds(0, used + 1)],
            send_sem=gather_send, recv_sem=gather_recv,
            device_id=(slab, *target), device_id_type=MESH)

    each(n, lambda o: gather_copy(o).start())
    gathered[me] = spread[c0]

    @pl.loop(0, outer)
    def _(m):
        at = pl.ds(pl.multiple_of(m * LANES, LANES), LANES)
        for rows in (lo, hi):
            pieces = [filt[c, rows, at] for c in range(chans)]
            for t in range(9):
                total = second_ref[t // 3, t % 3, 0] * pieces[0]
                for c in range(1, chans):
                    total = total + second_ref[t // 3, t % 3, c] * pieces[c]
                mixed[t, rows, at] = total

    sides = []
    for j in range(3):
        total = mixed[3 + j]
        for i in (0, 2):
            total = total + pltpu.roll(mixed[3 * i + j], -(i - 1) * rq % both, 0)
        sides.append(total)
    image = sides[1] + from_left(sides[0]) + from_right(sides[2])
    for a in range(angles):
        sino_ref[a] = image[a * rq : (a + 1) * rq]

    all_of(spreads, spreads, gather_send, gather_recv).wait_recv()
    sums = gathered[0, used : used + 1, :]
    for d in range(1, n):
        sums = sums + gathered[d, used : used + 1, :]
    for l in range(chans_dev):
        for i in range(3):
            at = l * SLOTS + 3 * i
            first_out_ref[i, l : l + 1, :] = sums[:, at : at + 3]
            second_out_ref[i, l : l + 1, :] = sums[:, at + 16 : at + 19]
        bias_out_ref[0:1, l : l + 1] = sums[:, l * SLOTS + 9 : l * SLOTS + 10]

    for m in range(outer):
        owner, at = m // per, m % per
        rz, rk, rc = owner // (team_k * ch_n), owner // ch_n % team_k, owner % ch_n
        pieces = [
            gathered[number((jz + rz, jk + rk, rc)), at * chans_dev : (at + 1) * chans_dev, :]
            for jz in range(0, ang_n, team_z) for jk in range(0, row_n, team_k)]
        taps_out_ref[:, cols(m)] = functools.reduce(lambda x, y: x + y, pieces)

    if ang_n > 1:
        sent = got.at[pl.ds(0, ang_n - 1), pl.ds(0, (rq + 2) * outer)]
        all_of(sent, sent, rows_send, rows_recv.at[0]).wait_send()
    if ch_n > 1:
        sent = all_taps.at[pl.ds(0, ch_n - 1)]
        all_of(sent, sent, taps_send, taps_recv).wait_send()
        sent = all_packed.at[pl.ds(0, ch_n - 1)]
        all_of(sent, sent, packed_send, packed_recv).wait_send()

    @pl.when(sends_top)
    def _():
        top_copy(z).wait_send()

    @pl.when(sends_bottom)
    def _():
        bottom_copy(z).wait_send()

    all_of(summed, summed, sum_send, sum_recv).wait_send()
    all_of(spreads, spreads, gather_send, gather_recv).wait_send()


def deliver(*refs):
    count = (len(refs) - 1) // 2
    sources, targets, sems = refs[:count], refs[count : 2 * count], refs[-1]
    copies = [pltpu.make_async_copy(sources[at], targets[at], sems.at[at]) for at in range(count)]
    for copy in copies:
        copy.start()
    for copy in copies:
        copy.wait()


def on_device(sizes, tables, projections, conv1_weight, conv1_bias, filter_taps, conv2_weight, cotangent):
    ang_n, row_n, ch_n = sizes
    n = ang_n * row_n * ch_n
    _, held, columns = projections.shape
    chans_dev = conv1_weight.shape[0]
    chans = chans_dev * ch_n
    _, angles, rq, _ = cotangent.shape
    outer = columns // LANES
    both = angles * rq
    block = outer * both // 2
    rp = padded_rows(rq)
    team_n = math.prod(team_sizes(sizes)) * ch_n
    slot = -(-(outer // team_n * chans_dev + 1) // 8) * 8
    f32 = jnp.float32
    vmem = pl.BlockSpec(memory_space=pltpu.VMEM)
    hbm = pl.BlockSpec(memory_space=pltpu.HBM)
    dma = pltpu.SemaphoreType.DMA
    wide = (both, columns)
    shapes = (
        jax.ShapeDtypeStruct((angles, rq, columns), f32),
        jax.ShapeDtypeStruct((3, chans_dev, 3), f32),
        jax.ShapeDtypeStruct((1, chans_dev), f32),
        jax.ShapeDtypeStruct((chans_dev, columns), f32),
        jax.ShapeDtypeStruct((3, chans_dev, 3), f32),
    )
    results = pl.pallas_call(
        functools.partial(kernel, sizes),
        out_shape=tuple(pltpu.VMEM(leaf.shape, f32) for leaf in shapes),
        in_specs=[hbm] * 9,
        out_specs=(vmem,) * 5,
        scratch_shapes=[
            pltpu.VMEM((held, columns), f32),
            pltpu.VMEM((3, chans_dev, 3), f32),
            pltpu.VMEM((1, chans_dev), f32),
            pltpu.VMEM((chans_dev, columns), f32),
            pltpu.VMEM((angles, rq, columns), f32),
            pltpu.VMEM(tables[0].shape, jnp.bfloat16),
            pltpu.VMEM(tables[1].shape, f32),
            pltpu.VMEM(tables[2].shape, f32),
            pltpu.VMEM(((held + 2) * outer, LANES), f32),
            pltpu.VMEM((chans_dev, LANES), f32),
            pltpu.VMEM((ch_n, 1, LANES), f32),
            pltpu.VMEM((ang_n, rp * outer, LANES), f32),
            pltpu.VMEM((ang_n, outer, LANES), f32),
            pltpu.VMEM((ang_n, outer, LANES), f32),
            pltpu.VMEM((ch_n, chans_dev, columns), f32),
            pltpu.VMEM((ch_n, chans_dev, LANES), f32),
            pltpu.SMEM((ch_n, chans_dev, LANES), f32),
            pltpu.SMEM((3, 3, chans), f32),
            pltpu.VMEM((9,) + wide, f32),
            pltpu.VMEM((chans * block, 2 * LANES), f32),
            pltpu.VMEM((chans * block, 2 * LANES), f32),
            pltpu.VMEM((block, 2 * LANES), f32),
            pltpu.VMEM(((chans + 1) * block, 2 * LANES), f32),
            pltpu.VMEM((chans,) + wide, f32),
            pltpu.VMEM((chans * both, columns), f32),
            pltpu.VMEM((chans * both, columns), f32),
            pltpu.VMEM((chans,) + wide, f32),
            pltpu.VMEM((chans, SLOTS, LANES), f32),
            pltpu.VMEM((9,) + wide, f32),
            pltpu.VMEM((angles * 6 * rp, columns), jnp.bfloat16),
            pltpu.VMEM((2 * chans * both, angles * 6 * rp), jnp.bfloat16),
            pltpu.VMEM((2 * chans * both, columns), jnp.bfloat16),
            pltpu.VMEM((outer, chans, LANES), f32),
            pltpu.VMEM((team_n, outer // team_n, chans, LANES), f32),
            pltpu.VMEM((ch_n, slot, LANES), f32),
            pltpu.VMEM((n, slot, LANES), f32),
            dma(()), dma((ang_n,)), dma((2,)), dma((2,)),
            dma(()), dma(()), dma(()), dma(()),
            dma(()), dma(()), dma(()), dma(()), dma((9,)), dma(()),
        ],
        compiler_params=pltpu.CompilerParams(
            collective_id=0, has_side_effects=True, vmem_limit_bytes=63 * 2**20
        ),
        name="tomography",
    )(
        projections[0], jnp.transpose(conv1_weight, (1, 0, 2)), conv1_bias[None], filter_taps,
        jnp.transpose(conv2_weight, (1, 2, 0)), cotangent[0], *tables,
    )
    image, first, bias, taps_out, second = pl.pallas_call(
        deliver,
        out_shape=shapes,
        in_specs=[vmem] * 5,
        out_specs=(hbm,) * 5,
        scratch_shapes=[dma((5,))],
        name="deliver",
    )(*[pltpu.with_memory_space_constraint(leaf, pltpu.VMEM) for leaf in results])
    return (
        image[None], jnp.transpose(first, (1, 0, 2)), bias[0], taps_out,
        jnp.transpose(second, (1, 0, 2)),
    )


def solution(mesh):
    sizes = tuple(mesh.shape[axis] for axis in ("ang", "row", "ch"))

    def whole(projections, conv1_weight, conv1_bias, filter_taps, conv2_weight, cotangent):
        angles, rq = cotangent.shape[1], cotangent.shape[2] // (sizes[0] * sizes[2])
        tables = (*make_tables(projections.shape[-1]), make_masks(angles, rq))

        def local(*arrays):
            return on_device(sizes, tuple(jnp.asarray(t) for t in tables), *arrays)

        return jax.shard_map(
            local,
            mesh=mesh,
            in_specs=(
                P(("slab", "ang"), "row", None),
                P("ch", None, None),
                P("ch"),
                P("ch", None),
                P(),
                P(("slab", "row"), None, ("ang", "ch"), None),
            ),
            out_specs=(
                P(("slab", "row"), None, ("ang", "ch"), None),
                P(("slab", "ch"), None, None),
                P(("slab", "ch")),
                P(("slab", "ch"), None),
                P(("slab", "ch"), None, None),
            ),
            check_vma=False,
        )(projections, conv1_weight, conv1_bias, filter_taps, conv2_weight, cotangent)

    return whole
```

```python
import functools
import math

import jax
import jax.numpy as jnp
import numpy as np
import ml_dtypes
from jax import lax
from jax.experimental import pallas as pl
from jax.experimental.pallas import tpu as pltpu
from jax.sharding import PartitionSpec as P

MESH = pl.DeviceIdType.MESH
LANES = 128
SLOTS = 32


def twisted(value, k, n, sign):
    re, im = value
    if k == 0:
        return value
    if 4 * k == n:
        return (-im, re) if sign > 0 else (im, -re)
    if 8 * k == n:
        half = math.sqrt(0.5)
        return (half * (re - sign * im), half * (im + sign * re))
    if 8 * k == 3 * n:
        half = math.sqrt(0.5)
        return (half * (-re - sign * im), half * (-im + sign * re))
    cos = math.cos(2 * math.pi * k / n)
    sin = sign * math.sin(2 * math.pi * k / n)
    return (cos * re - sin * im, cos * im + sin * re)


def short_dft(values, sign):
    n = len(values)
    if n == 1:
        return values
    even = short_dft(values[0::2], sign)
    odd = short_dft(values[1::2], sign)
    low, high = [], []
    for k in range(n // 2):
        re, im = twisted(odd[k], k, n, sign)
        low.append((even[k][0] + re, even[k][1] + im))
        high.append((even[k][0] - re, even[k][1] - im))
    return low + high


def split_high_low(table):
    high = table.astype(ml_dtypes.bfloat16)
    low = (table - high.astype(np.float64)).astype(ml_dtypes.bfloat16)
    return high, low


def make_tables(length):
    outer = length // LANES
    index = np.arange(LANES)
    inner = 2 * np.pi * (np.outer(index, index) % LANES) / LANES
    cos, sin = np.cos(inner), np.sin(inner)
    forward = np.block([[cos, -sin], [sin, cos]])
    inverse = np.block([[cos, sin], [-sin, cos]]) / length
    twist = 2 * np.pi * np.outer(np.arange(outer), index) / length
    twist = np.repeat(twist, 8, axis=0)
    tables = np.stack([*split_high_low(forward), *split_high_low(inverse)])
    turns = np.stack([np.cos(twist), np.sin(twist)]).astype(np.float32)
    return tables, turns


def padded_rows(rq):
    return -(-(rq + 3) // 8) * 8


def make_masks(angles, rq):
    rp = padded_rows(rq)
    near = angles // 2
    masks = np.zeros((11, angles, rq, near, 2, 3, rp), np.float32)
    for a in range(angles):
        for r in range(rq):
            for t in range(9):
                masks[t, a, r, a % near, :, t % 3, r + t // 3] = 1
            masks[9, a, r, a % near, 0, 1, rq + 2] = 1
            masks[10, a, r, :, 0] = 1
    masks = masks.reshape(11, angles * rq, near * 6 * rp)
    return np.pad(masks, ((0, 0), (0, 0), (0, -masks.shape[2] % LANES)))


def fold_rows(values):
    count, lines = len(values), values[0].shape[0]
    line = lax.broadcasted_iota(jnp.int32, values[0].shape, 0)
    step = lines // 2
    while step >= count:
        values = [value + pltpu.roll(value, step, 0) for value in values]
        step //= 2
    while step:
        first = (line & step) == 0
        values = [
            jnp.where(first, a, b)
            + jnp.where(first, pltpu.roll(a, lines - step, 0), pltpu.roll(b, step, 0))
            for a, b in zip(values[:step], values[step:])
        ]
        step //= 2
    return values[0]


def multiply(ref, start, rows, tables_ref, which):
    values = ref[pl.ds(start, rows), :]
    high = values.astype(jnp.bfloat16)
    low = (values - high.astype(jnp.float32)).astype(jnp.bfloat16)
    dot = functools.partial(jnp.dot, preferred_element_type=jnp.float32)
    table_high = tables_ref[which]
    ref[pl.ds(start, rows), :] = (
        dot(high, table_high) + dot(low, table_high) + dot(high, tables_ref[which + 1])
    )


def team_sizes(sizes):
    return tuple(2 if size % 2 == 0 else 1 for size in sizes[:2])


def each(count, body):
    if count <= 32:
        for o in reversed(range(1, count)):
            body(o)
    else:
        pl.loop(1, count)(body)


def kernel(
    sizes,
    proj_hbm, first_hbm, bias_hbm, taps_hbm, second_hbm, cot_hbm, tables_hbm, turns_hbm, masks_hbm,
    sino_ref, first_out_ref, bias_out_ref, taps_out_ref, second_out_ref,
    proj_ref, first_vmem, bias_vmem, taps_ref, cot_ref, tables_ref, turns_ref, masks_ref,
    rows_ref, packed_ref, small_own,
    got, top, bottom, all_taps, all_packed, first_ref, second_ref,
    cot_shift, spec_back, spec_hidden, spec_taps, work,
    back, hidden_ref, gate_ref, filt, partial, mixed, lines_ref, first_matrix, grads_ref,
    outgoing, incoming, spread, gathered,
    rows_send, rows_recv, edge_send, edge_recv, taps_send, taps_recv,
    packed_send, packed_recv, sum_send, sum_recv, gather_send, gather_recv, load_sem, local_sem,
):
    ang_n, row_n, ch_n = sizes
    n = ang_n * row_n * ch_n
    angles, rq, columns = cot_ref.shape
    chans = second_ref.shape[2]
    chans_dev = taps_ref.shape[0]
    held = proj_ref.shape[0]
    both = angles * rq
    half = both // 2
    outer = columns // LANES
    block = outer * half
    depth = lines_ref.shape[0] // 2
    rp = depth // (3 * angles)
    team_n = incoming.shape[0]
    team_z, team_k = team_sizes(sizes)
    per = outer // team_n
    slab = lax.axis_index("slab")
    z, k, c0 = lax.axis_index("ang"), lax.axis_index("row"), lax.axis_index("ch")
    me = (z * row_n + k) * ch_n + c0

    paired = all(size & (size - 1) == 0 for size in sizes)

    def other(at, o, size):
        return at ^ o if paired else (at + o) % size

    def origin_of(at, o, size):
        return at ^ o if paired else (at + size - o) % size

    def partner(o):
        oz, ok, oc = o // (row_n * ch_n), o // ch_n % row_n, o % ch_n
        return other(z, oz, ang_n), other(k, ok, row_n), other(c0, oc, ch_n)

    def number(at):
        return (at[0] * row_n + at[1]) * ch_n + at[2]

    barrier = pltpu.get_barrier_semaphore()
    loads = [
        pltpu.make_async_copy(source, target, load_sem.at[at])
        for at, (source, target) in enumerate((
            (proj_hbm, proj_ref), (first_hbm, first_vmem), (bias_hbm, bias_vmem),
            (taps_hbm, taps_ref), (cot_hbm, cot_ref), (tables_hbm, tables_ref),
            (turns_hbm, turns_ref), (second_hbm, second_ref),
            (masks_hbm, masks_ref)))
    ]
    loads[0].start()
    each(n, lambda o: pl.semaphore_signal(
        barrier, inc=1, device_id=(slab, *partner(o)), device_id_type=MESH))
    for load in loads[1:]:
        load.start()

    def cols(m):
        return slice(m * LANES, (m + 1) * LANES)

    edge = jnp.zeros((outer, LANES), jnp.float32)
    rows_ref[0:outer, :] = edge
    rows_ref[(held + 1) * outer : (held + 2) * outer, :] = edge
    packed_ref[...] = jnp.zeros(packed_ref.shape, jnp.float32)
    loads[0].wait()
    for at in range(0, held, 8):
        for m in range(outer):
            rows_ref[pl.ds((at + 1) * outer + m, 8, stride=outer), :] = proj_ref[at : at + 8, cols(m)]
    loads[1].wait()
    loads[2].wait()
    for i in range(3):
        packed_ref[:, 3 * i : 3 * i + 3] = first_vmem[i]
    for l in range(chans_dev):
        packed_ref[l : l + 1, 9:10] = bias_vmem[0:1, l : l + 1]
    loads[3].wait()
    pl.semaphore_wait(barrier, n - 1)

    def all_of(source, target, send_sem, recv_sem):
        return pltpu.make_async_remote_copy(
            src_ref=source, dst_ref=target, send_sem=send_sem, recv_sem=recv_sem,
            device_id=(slab, *partner(1)), device_id_type=MESH)

    def rows_copy(o, slot, target):
        start = pl.multiple_of((target * ch_n + c0) * rq * outer, outer)
        return pltpu.make_async_remote_copy(
            src_ref=rows_ref.at[pl.ds(start, (rq + 2) * outer)], dst_ref=got.at[slot, pl.ds(0, (rq + 2) * outer)],
            send_sem=rows_send, recv_sem=rows_recv.at[slot],
            device_id=(slab, target, k, c0), device_id_type=MESH)

    def taps_copy(o, slot, target):
        return pltpu.make_async_remote_copy(
            src_ref=taps_ref, dst_ref=all_taps.at[slot],
            send_sem=taps_send, recv_sem=taps_recv,
            device_id=(slab, z, k, target), device_id_type=MESH)

    def packed_copy(o, slot, target):
        return pltpu.make_async_remote_copy(
            src_ref=packed_ref, dst_ref=all_packed.at[slot],
            send_sem=packed_send, recv_sem=packed_recv,
            device_id=(slab, z, k, target), device_id_type=MESH)

    def top_copy(slot):
        return pltpu.make_async_remote_copy(
            src_ref=rows_ref.at[pl.ds(held * outer, outer)], dst_ref=top.at[slot],
            send_sem=edge_send.at[0], recv_sem=edge_recv.at[0],
            device_id=(slab, 0, (k + 1) % row_n, 0), device_id_type=MESH)

    def bottom_copy(slot):
        return pltpu.make_async_remote_copy(
            src_ref=rows_ref.at[pl.ds(outer, outer)], dst_ref=bottom.at[slot],
            send_sem=edge_send.at[1], recv_sem=edge_recv.at[1],
            device_id=(slab, ang_n - 1, (k + row_n - 1) % row_n, ch_n - 1), device_id_type=MESH)

    for o in reversed(range(1, ang_n)):
        rows_copy(o, z, other(z, o, ang_n)).start()
    for o in range(1, ch_n):
        taps_copy(o, c0, (c0 + o) % ch_n).start()
        packed_copy(o, c0, (c0 + o) % ch_n).start()
    sends_top = jnp.logical_and(c0 == 0, k < row_n - 1)
    sends_bottom = jnp.logical_and(c0 == ch_n - 1, k > 0)

    @pl.when(sends_top)
    def _():
        top_copy(z).start()

    @pl.when(sends_bottom)
    def _():
        bottom_copy(z).start()

    mine_at = pl.multiple_of((z * ch_n + c0) * rq * outer, outer)
    for a in range(ang_n):
        got[a, (rq + 2) * outer : (rq + 3) * outer, :] = jnp.ones((outer, LANES), jnp.float32)
        if rp > rq + 3:
            rest = (rp - rq - 3) * outer
            got[a, (rq + 3) * outer : rp * outer, :] = jnp.zeros((rest, LANES), jnp.float32)
    got[z, 0 : (rq + 2) * outer, :] = rows_ref[pl.ds(mine_at, (rq + 2) * outer), :]
    all_taps[c0] = taps_ref[...]
    all_packed[c0] = packed_ref[...]

    def from_left(x):
        column = lax.broadcasted_iota(jnp.int32, x.shape, 1)
        return jnp.where(column == 0, 0.0, pltpu.roll(x, 1, 1))

    def from_right(x):
        column = lax.broadcasted_iota(jnp.int32, x.shape, 1)
        return jnp.where(column == columns - 1, 0.0, pltpu.roll(x, columns - 1, 1))

    lo, hi = slice(0, half), slice(half, both)
    re_l, im_l = slice(0, LANES), slice(LANES, 2 * LANES)

    loads[4].wait()
    upstream = jnp.concatenate([cot_ref[a] for a in range(angles)], axis=0)
    for i in range(3):
        shift = (i - 1) * rq % both
        turned = pltpu.roll(upstream, shift, 0) if shift else upstream
        cot_shift[3 * i] = from_right(turned)
        cot_shift[3 * i + 1] = turned
        cot_shift[3 * i + 2] = from_left(turned)

    def store_forward(ref, start, values):
        for q, (re, im) in enumerate(short_dft(values, -1)):
            part = slice(q * half, (q + 1) * half)
            cos, sin = turns_ref[0, part, :], turns_ref[1, part, :]
            rows = pl.ds(start + q * half, half)
            ref[rows, re_l] = re * cos + im * sin
            ref[rows, im_l] = im * cos - re * sin

    def load_inverse(ref, start):
        values = []
        for q in range(outer):
            part = slice(q * half, (q + 1) * half)
            cos, sin = turns_ref[0, part, :], turns_ref[1, part, :]
            rows = pl.ds(start + q * half, half)
            re, im = ref[rows, re_l], ref[rows, im_l]
            values.append((re * cos - im * sin, im * cos + re * sin))
        return short_dft(values, 1)

    def start_of(c):
        return pl.multiple_of(c * block, block)

    loads[5].wait()
    loads[6].wait()
    loads[7].wait()

    @pl.loop(0, chans)
    def _(c):
        weights = [second_ref[t // 3, t % 3, c] for t in range(9)]
        values = []
        for m in range(outer):
            pair = []
            for rows in (lo, hi):
                total = weights[0] * cot_shift[0, rows, cols(m)]
                for t in range(1, 9):
                    total = total + weights[t] * cot_shift[t, rows, cols(m)]
                pair.append(total)
            values.append(tuple(pair))
        store_forward(spec_back, start_of(c), values)

    step = 4 * block
    for s in range(0, chans * block, step):
        multiply(spec_back, s, step, tables_ref, 0)

    if ch_n > 1:
        all_of(all_taps.at[pl.ds(0, ch_n - 1)], all_taps.at[pl.ds(0, ch_n - 1)], taps_send, taps_recv).wait_recv()
        all_of(all_packed.at[pl.ds(0, ch_n - 1)], all_packed.at[pl.ds(0, ch_n - 1)], packed_send, packed_recv).wait_recv()
    load_weights = pltpu.make_async_copy(all_packed, first_ref, local_sem)
    load_weights.start()
    taps = jnp.concatenate([all_taps[h] for h in range(ch_n)], axis=0)
    zero = jnp.zeros((chans, LANES), jnp.float32)
    store_forward(spec_taps, 0, [(taps[:, cols(m)], zero) for m in range(outer)])
    multiply(spec_taps, 0, block, tables_ref, 0)

    def tap_row(q, c):
        row = spec_taps[pl.ds(q * half + c, 1), :]
        row = jnp.broadcast_to(row, (half, 2 * LANES))
        return row[:, re_l], row[:, im_l]

    @pl.loop(0, chans)
    def _(c):
        for q in range(outer):
            tr, ti = tap_row(q, c)
            rows = pl.ds(start_of(c) + q * half, half)
            gr, gi = spec_back[rows, re_l], spec_back[rows, im_l]
            work[rows, re_l] = tr * gr - ti * gi
            work[rows, im_l] = tr * gi + ti * gr

    for s in range(0, chans * block, step):
        multiply(work, s, step, tables_ref, 2)

    @pl.loop(0, chans)
    def _(c):
        for m, (re, im) in enumerate(load_inverse(work, start_of(c))):
            back[c, lo, cols(m)] = re
            back[c, hi, cols(m)] = im

    load_weights.wait()
    loads[8].wait()
    for c in range(0, chans, 2):
        totals = []
        for e in (c, c + 1):
            h, l = e // chans_dev, e % chans_dev
            total = first_ref[h, l, 9] * masks_ref[9]
            for t in range(9):
                total = total + first_ref[h, l, t] * masks_ref[t]
            totals.append(total)
        for side, rows in enumerate((lo, hi)):
            total = jnp.concatenate([value[rows, 0:depth] for value in totals], axis=0)
            high = total.astype(jnp.bfloat16)
            low = (total - high.astype(jnp.float32)) * masks_ref[10, :, 0:depth]
            first_matrix[side, c * half : (c + 2) * half, :] = high
            first_matrix[side, (chans + c) * half : (chans + c + 2) * half, :] = low.astype(jnp.bfloat16)

    has_top = jnp.logical_and(jnp.logical_and(z == 0, c0 == 0), k > 0)
    has_bottom = jnp.logical_and(jnp.logical_and(z == ang_n - 1, c0 == ch_n - 1), k < row_n - 1)

    @pl.when(has_top)
    def _():
        all_of(top, top, edge_send.at[0], edge_recv.at[0]).wait_recv()

    @pl.when(has_bottom)
    def _():
        all_of(bottom, bottom, edge_send.at[1], edge_recv.at[1]).wait_recv()

    def prepare(a):
        @pl.when(has_top)
        def _():
            got[a, 0:outer, :] = top[a]

        @pl.when(has_bottom)
        def _():
            got[a, (rq + 1) * outer : (rq + 2) * outer, :] = bottom[a]

        centre = jnp.concatenate(
            [got[a, pl.ds(m, rp, stride=outer), :] for m in range(outer)], axis=1)
        lines = jnp.concatenate([from_left(centre), centre, from_right(centre)], axis=0)
        high = lines.astype(jnp.bfloat16).astype(jnp.float32)
        at = pl.multiple_of(a * 6 * rp, 6 * rp)
        lines_ref[pl.ds(at, 6 * rp), :] = jnp.concatenate(
            [high, lines - high], axis=0).astype(jnp.bfloat16)

    dot = functools.partial(jnp.dot, preferred_element_type=jnp.float32)

    def activate(side):
        at = pl.ds(pl.multiple_of(side * chans * half, chans * half), chans * half)
        rows = pl.ds(pl.multiple_of(side * depth, depth), depth)
        for start in range(0, columns, 2 * LANES):
            chunk = slice(start, start + 2 * LANES)
            total = dot(first_matrix[side], lines_ref[rows, chunk])
            total = total[0 : chans * half] + total[chans * half : 2 * chans * half]
            gate = 0.5 + 0.5 * jnp.tanh(0.5 * total)
            gate_ref[at, chunk] = gate
            hidden_ref[at, chunk] = total * gate

    near_n = ang_n // 2
    near = z // near_n
    prepare(z)
    for side, first in ((near, 1), (1 - near, 0)):
        for o in range(first, near_n):
            origin = side * near_n + (z % near_n + o) % near_n
            rows_copy(o, origin, origin).wait_recv()
            prepare(origin)
        activate(side)

    group = chans // 2
    line_of = lax.broadcasted_iota(jnp.int32, (half, LANES), 0)

    def cross(first):
        for q in range(outer):
            at = slice(chans * block + q * half, chans * block + (q + 1) * half)
            reals, imags = [], []
            for c in range(first, first + group):
                line = slice(c * block + q * half, c * block + (q + 1) * half)
                gr, gi = spec_back[line, re_l], spec_back[line, im_l]
                hr, hi_ = spec_hidden[line, re_l], spec_hidden[line, im_l]
                reals.append(gr * hr + gi * hi_)
                imags.append(gr * hi_ - gi * hr)
            for side, values in ((re_l, reals), (im_l, imags)):
                value = fold_rows(values)
                work[at, side] = value if first == 0 else jnp.where(line_of < group, work[at, side], value)

    for c in range(chans):
        values = [
            (hidden_ref[c * half : (c + 1) * half, cols(m)],
             hidden_ref[(chans + c) * half : (chans + c + 1) * half, cols(m)])
            for m in range(outer)]
        store_forward(spec_hidden, c * block, values)
        if c + 1 == group:
            multiply(spec_hidden, 0, group * block, tables_ref, 0)
    cross(0)
    multiply(spec_hidden, group * block, group * block, tables_ref, 0)
    cross(group)

    multiply(work, chans * block, block, tables_ref, 2)
    for m, (re, im) in enumerate(load_inverse(work, chans * block)):
        outgoing[m] = re

    def folded(value):
        return jnp.sum(value, axis=0, keepdims=True)

    def mate(o):
        oz, ok, oc = o // (team_k * ch_n), o // ch_n % team_k, o % ch_n
        there_z = z // team_z * team_z + (z + oz) % team_z
        there_k = k // team_k * team_k + (k + ok) % team_k
        return there_z, there_k, (c0 + oc) % ch_n

    def rank(at):
        return (at[0] % team_z * team_k + at[1] % team_k) * ch_n + at[2]

    def sum_copy(o):
        target = mate(o)
        return pltpu.make_async_remote_copy(
            src_ref=outgoing.at[pl.ds(rank(target) * per, per)], dst_ref=incoming.at[o],
            send_sem=sum_send, recv_sem=sum_recv,
            device_id=(slab, *target), device_id_type=MESH)

    each(team_n, lambda o: sum_copy(o).start())

    @pl.loop(0, chans)
    def _(c):
        for q in range(outer):
            tr, ti = tap_row(q, c)
            rows = pl.ds(start_of(c) + q * half, half)
            hr, hi_ = spec_hidden[rows, re_l], spec_hidden[rows, im_l]
            work[rows, re_l] = tr * hr + ti * hi_
            work[rows, im_l] = tr * hi_ - ti * hr

    for s in range(0, chans * block, step):
        multiply(work, s, step, tables_ref, 2)

    partial[...] = jnp.zeros(partial.shape, jnp.float32)

    @pl.loop(0, chans // 2)
    def _(c):
        for side, rows in enumerate((lo, hi)):
            at = pl.ds(pl.multiple_of(side * chans * half + c * both, both), both)
            at_high = pl.ds(pl.multiple_of(c * both, both), both)
            at_low = pl.ds(pl.multiple_of(chans * half + c * both, both), both)
            for m in range(outer):
                gate = gate_ref[at, cols(m)]
                grad = jnp.concatenate([back[2 * c, rows, cols(m)], back[2 * c + 1, rows, cols(m)]], axis=0)
                grad = grad * (gate + hidden_ref[at, cols(m)] * (1.0 - gate))
                high = grad.astype(jnp.bfloat16)
                grads_ref[side, at_high, cols(m)] = high
                grads_ref[side, at_low, cols(m)] = (grad - high.astype(jnp.float32)).astype(jnp.bfloat16)

    wide = masks_ref.shape[2]
    totals = []
    for side in range(2):
        total = lax.dot_general(
            grads_ref[side], lines_ref[side * depth : (side + 1) * depth, :], (((1,), (1,)), ((), ())),
            preferred_element_type=jnp.float32)
        total = total[0 : chans * half] + total[chans * half : 2 * chans * half]
        if wide > depth:
            total = jnp.concatenate([total, jnp.zeros((chans * half, wide - depth), jnp.float32)], axis=1)
        totals.append(total)
    for c in range(chans):
        values = []
        for t in range(10):
            value = totals[0][c * half : (c + 1) * half] * masks_ref[t, lo, :]
            value = value + totals[1][c * half : (c + 1) * half] * masks_ref[t, hi, :]
            values.append(functools.reduce(
                lambda x, y: x + y, [value[:, at : at + LANES] for at in range(0, wide, LANES)]))
        partial[c, 0:8, :] = fold_rows(values[0:8])
        partial[c, 8:9, :] = folded(values[8])
        partial[c, 9:10, :] = folded(values[9])

    @pl.loop(0, chans)
    def _(c):
        sums = [jnp.zeros((half, LANES), jnp.float32) for _ in range(9)]
        for m, (re, im) in enumerate(load_inverse(work, start_of(c))):
            filt[c, lo, cols(m)] = re
            filt[c, hi, cols(m)] = im
            for t in range(9):
                sums[t] = sums[t] + re * cot_shift[t, lo, cols(m)] + im * cot_shift[t, hi, cols(m)]
        for t in range(9):
            partial[c, 16 + t : 17 + t, :] = folded(sums[t])

    small = lax.dot_general(
        jnp.ones((8, LANES), jnp.float32), partial[...].reshape(chans * SLOTS, LANES),
        (((1,), (1,)), ((), ())),
        precision=lax.Precision.HIGHEST, preferred_element_type=jnp.float32)
    width = chans_dev * SLOTS
    for h in range(ch_n):
        small_own[h] = small[0:1, h * width : (h + 1) * width]

    mine = pl.multiple_of(rank((z, k, c0)) * per, per)
    total = outgoing[pl.ds(mine, per)]
    summed = incoming.at[pl.ds(1, team_n - 1)]
    all_of(summed, summed, sum_send, sum_recv).wait_recv()
    for o in range(1, team_n):
        total = total + incoming[o]
    used = per * chans_dev
    for h in range(ch_n):
        for p in range(per):
            at = slice(p * chans_dev, (p + 1) * chans_dev)
            spread[h, at, :] = total[p, h * chans_dev : (h + 1) * chans_dev]
        spread[h, used : used + 1, :] = small_own[h]
    spreads = gathered.at[pl.ds(0, n - 1), pl.ds(0, used + 1)]

    def gather_copy(o):
        target = partner(o)
        return pltpu.make_async_remote_copy(
            src_ref=spread.at[target[2], pl.ds(0, used + 1)], dst_ref=gathered.at[me, pl.ds(0, used + 1)],
            send_sem=gather_send, recv_sem=gather_recv,
            device_id=(slab, *target), device_id_type=MESH)

    each(n, lambda o: gather_copy(o).start())
    gathered[me] = spread[c0]

    @pl.loop(0, outer)
    def _(m):
        at = pl.ds(pl.multiple_of(m * LANES, LANES), LANES)
        for rows in (lo, hi):
            pieces = [filt[c, rows, at] for c in range(chans)]
            for t in range(9):
                total = second_ref[t // 3, t % 3, 0] * pieces[0]
                for c in range(1, chans):
                    total = total + second_ref[t // 3, t % 3, c] * pieces[c]
                mixed[t, rows, at] = total

    sides = []
    for j in range(3):
        total = mixed[3 + j]
        for i in (0, 2):
            total = total + pltpu.roll(mixed[3 * i + j], -(i - 1) * rq % both, 0)
        sides.append(total)
    image = sides[1] + from_left(sides[0]) + from_right(sides[2])
    for a in range(angles):
        sino_ref[a] = image[a * rq : (a + 1) * rq]

    all_of(spreads, spreads, gather_send, gather_recv).wait_recv()
    sums = gathered[0, used : used + 1, :]
    for d in range(1, n):
        sums = sums + gathered[d, used : used + 1, :]
    for l in range(chans_dev):
        for i in range(3):
            at = l * SLOTS + 3 * i
            first_out_ref[i, l : l + 1, :] = sums[:, at : at + 3]
            second_out_ref[i, l : l + 1, :] = sums[:, at + 16 : at + 19]
        bias_out_ref[0:1, l : l + 1] = sums[:, l * SLOTS + 9 : l * SLOTS + 10]

    for m in range(outer):
        owner, at = m // per, m % per
        rz, rk, rc = owner // (team_k * ch_n), owner // ch_n % team_k, owner % ch_n
        pieces = [
            gathered[number((jz + rz, jk + rk, rc)), at * chans_dev : (at + 1) * chans_dev, :]
            for jz in range(0, ang_n, team_z) for jk in range(0, row_n, team_k)]
        taps_out_ref[:, cols(m)] = functools.reduce(lambda x, y: x + y, pieces)

    if ang_n > 1:
        sent = got.at[pl.ds(0, ang_n - 1), pl.ds(0, (rq + 2) * outer)]
        all_of(sent, sent, rows_send, rows_recv.at[0]).wait_send()
    if ch_n > 1:
        sent = all_taps.at[pl.ds(0, ch_n - 1)]
        all_of(sent, sent, taps_send, taps_recv).wait_send()
        sent = all_packed.at[pl.ds(0, ch_n - 1)]
        all_of(sent, sent, packed_send, packed_recv).wait_send()

    @pl.when(sends_top)
    def _():
        top_copy(z).wait_send()

    @pl.when(sends_bottom)
    def _():
        bottom_copy(z).wait_send()

    all_of(summed, summed, sum_send, sum_recv).wait_send()
    all_of(spreads, spreads, gather_send, gather_recv).wait_send()


def deliver(*refs):
    count = (len(refs) - 1) // 2
    sources, targets, sems = refs[:count], refs[count : 2 * count], refs[-1]
    copies = [pltpu.make_async_copy(sources[at], targets[at], sems.at[at]) for at in range(count)]
    for copy in copies:
        copy.start()
    for copy in copies:
        copy.wait()


def on_device(sizes, tables, projections, conv1_weight, conv1_bias, filter_taps, conv2_weight, cotangent):
    ang_n, row_n, ch_n = sizes
    n = ang_n * row_n * ch_n
    _, held, columns = projections.shape
    chans_dev = conv1_weight.shape[0]
    chans = chans_dev * ch_n
    _, angles, rq, _ = cotangent.shape
    outer = columns // LANES
    both = angles * rq
    block = outer * both // 2
    rp = padded_rows(rq)
    team_n = math.prod(team_sizes(sizes)) * ch_n
    slot = -(-(outer // team_n * chans_dev + 1) // 8) * 8
    f32 = jnp.float32
    vmem = pl.BlockSpec(memory_space=pltpu.VMEM)
    hbm = pl.BlockSpec(memory_space=pltpu.HBM)
    dma = pltpu.SemaphoreType.DMA
    wide = (both, columns)
    shapes = (
        jax.ShapeDtypeStruct((angles, rq, columns), f32),
        jax.ShapeDtypeStruct((3, chans_dev, 3), f32),
        jax.ShapeDtypeStruct((1, chans_dev), f32),
        jax.ShapeDtypeStruct((chans_dev, columns), f32),
        jax.ShapeDtypeStruct((3, chans_dev, 3), f32),
    )
    results = pl.pallas_call(
        functools.partial(kernel, sizes),
        out_shape=tuple(pltpu.VMEM(leaf.shape, f32) for leaf in shapes),
        in_specs=[hbm] * 9,
        out_specs=(vmem,) * 5,
        scratch_shapes=[
            pltpu.VMEM((held, columns), f32),
            pltpu.VMEM((3, chans_dev, 3), f32),
            pltpu.VMEM((1, chans_dev), f32),
            pltpu.VMEM((chans_dev, columns), f32),
            pltpu.VMEM((angles, rq, columns), f32),
            pltpu.VMEM(tables[0].shape, jnp.bfloat16),
            pltpu.VMEM(tables[1].shape, f32),
            pltpu.VMEM(tables[2].shape, f32),
            pltpu.VMEM(((held + 2) * outer, LANES), f32),
            pltpu.VMEM((chans_dev, LANES), f32),
            pltpu.VMEM((ch_n, 1, LANES), f32),
            pltpu.VMEM((ang_n, rp * outer, LANES), f32),
            pltpu.VMEM((ang_n, outer, LANES), f32),
            pltpu.VMEM((ang_n, outer, LANES), f32),
            pltpu.VMEM((ch_n, chans_dev, columns), f32),
            pltpu.VMEM((ch_n, chans_dev, LANES), f32),
            pltpu.SMEM((ch_n, chans_dev, LANES), f32),
            pltpu.SMEM((3, 3, chans), f32),
            pltpu.VMEM((9,) + wide, f32),
            pltpu.VMEM((chans * block, 2 * LANES), f32),
            pltpu.VMEM((chans * block, 2 * LANES), f32),
            pltpu.VMEM((block, 2 * LANES), f32),
            pltpu.VMEM(((chans + 1) * block, 2 * LANES), f32),
            pltpu.VMEM((chans,) + wide, f32),
            pltpu.VMEM((chans * both, columns), f32),
            pltpu.VMEM((chans * both, columns), f32),
            pltpu.VMEM((chans,) + wide, f32),
            pltpu.VMEM((chans, SLOTS, LANES), f32),
            pltpu.VMEM((9,) + wide, f32),
            pltpu.VMEM((angles * 6 * rp, columns), jnp.bfloat16),
            pltpu.VMEM((2, chans * both, angles * 3 * rp), jnp.bfloat16),
            pltpu.VMEM((2, chans * both, columns), jnp.bfloat16),
            pltpu.VMEM((outer, chans, LANES), f32),
            pltpu.VMEM((team_n, outer // team_n, chans, LANES), f32),
            pltpu.VMEM((ch_n, slot, LANES), f32),
            pltpu.VMEM((n, slot, LANES), f32),
            dma(()), dma((ang_n,)), dma((2,)), dma((2,)),
            dma(()), dma(()), dma(()), dma(()),
            dma(()), dma(()), dma(()), dma(()), dma((9,)), dma(()),
        ],
        compiler_params=pltpu.CompilerParams(
            collective_id=0, has_side_effects=True, vmem_limit_bytes=63 * 2**20
        ),
        name="tomography",
    )(
        projections[0], jnp.transpose(conv1_weight, (1, 0, 2)), conv1_bias[None], filter_taps,
        jnp.transpose(conv2_weight, (1, 2, 0)), cotangent[0], *tables,
    )
    image, first, bias, taps_out, second = pl.pallas_call(
        deliver,
        out_shape=shapes,
        in_specs=[vmem] * 5,
        out_specs=(hbm,) * 5,
        scratch_shapes=[dma((5,))],
        name="deliver",
    )(*[pltpu.with_memory_space_constraint(leaf, pltpu.VMEM) for leaf in results])
    return (
        image[None], jnp.transpose(first, (1, 0, 2)), bias[0], taps_out,
        jnp.transpose(second, (1, 0, 2)),
    )


def solution(mesh):
    sizes = tuple(mesh.shape[axis] for axis in ("ang", "row", "ch"))

    def whole(projections, conv1_weight, conv1_bias, filter_taps, conv2_weight, cotangent):
        angles, rq = cotangent.shape[1], cotangent.shape[2] // (sizes[0] * sizes[2])
        tables = (*make_tables(projections.shape[-1]), make_masks(angles, rq))

        def local(*arrays):
            return on_device(sizes, tuple(jnp.asarray(t) for t in tables), *arrays)

        return jax.shard_map(
            local,
            mesh=mesh,
            in_specs=(
                P(("slab", "ang"), "row", None),
                P("ch", None, None),
                P("ch"),
                P("ch", None),
                P(),
                P(("slab", "row"), None, ("ang", "ch"), None),
            ),
            out_specs=(
                P(("slab", "row"), None, ("ang", "ch"), None),
                P(("slab", "ch"), None, None),
                P(("slab", "ch")),
                P(("slab", "ch"), None),
                P(("slab", "ch"), None, None),
            ),
            check_vma=False,
        )(projections, conv1_weight, conv1_bias, filter_taps, conv2_weight, cotangent)

    return whole
```

```python
import functools
import math

import jax
import jax.numpy as jnp
import numpy as np
import ml_dtypes
from jax import lax
from jax.experimental import pallas as pl
from jax.experimental.pallas import tpu as pltpu
from jax.sharding import PartitionSpec as P

MESH = pl.DeviceIdType.MESH
LANES = 128
SLOTS = 32


def twisted(value, k, n, sign):
    re, im = value
    if k == 0:
        return value
    if 4 * k == n:
        return (-im, re) if sign > 0 else (im, -re)
    if 8 * k == n:
        half = math.sqrt(0.5)
        return (half * (re - sign * im), half * (im + sign * re))
    if 8 * k == 3 * n:
        half = math.sqrt(0.5)
        return (half * (-re - sign * im), half * (-im + sign * re))
    cos = math.cos(2 * math.pi * k / n)
    sin = sign * math.sin(2 * math.pi * k / n)
    return (cos * re - sin * im, cos * im + sin * re)


def short_dft(values, sign):
    n = len(values)
    if n == 1:
        return values
    even = short_dft(values[0::2], sign)
    odd = short_dft(values[1::2], sign)
    low, high = [], []
    for k in range(n // 2):
        re, im = twisted(odd[k], k, n, sign)
        low.append((even[k][0] + re, even[k][1] + im))
        high.append((even[k][0] - re, even[k][1] - im))
    return low + high


def split_high_low(table):
    high = table.astype(ml_dtypes.bfloat16)
    low = (table - high.astype(np.float64)).astype(ml_dtypes.bfloat16)
    return high, low


def make_tables(length):
    outer = length // LANES
    index = np.arange(LANES)
    inner = 2 * np.pi * (np.outer(index, index) % LANES) / LANES
    cos, sin = np.cos(inner), np.sin(inner)
    forward = np.block([[cos, -sin], [sin, cos]])
    inverse = np.block([[cos, sin], [-sin, cos]]) / length
    twist = 2 * np.pi * np.outer(np.arange(outer), index) / length
    twist = np.repeat(twist, 8, axis=0)
    tables = np.stack([*split_high_low(forward), *split_high_low(inverse)])
    turns = np.stack([np.cos(twist), np.sin(twist)]).astype(np.float32)
    return tables, turns


def padded_rows(rq):
    return -(-(rq + 3) // 8) * 8


def make_masks(angles, rq):
    rp = padded_rows(rq)
    near = angles // 2
    masks = np.zeros((11, angles, rq, near, 2, 3, rp), np.float32)
    for a in range(angles):
        for r in range(rq):
            for t in range(9):
                masks[t, a, r, a % near, :, t % 3, r + t // 3] = 1
            masks[9, a, r, a % near, 0, 1, rq + 2] = 1
            masks[10, a, r, :, 0] = 1
    masks = masks.reshape(11, angles * rq, near * 6 * rp)
    return np.pad(masks, ((0, 0), (0, 0), (0, -masks.shape[2] % LANES)))


def fold_rows(values):
    count, lines = len(values), values[0].shape[0]
    line = lax.broadcasted_iota(jnp.int32, values[0].shape, 0)
    step = lines // 2
    while step >= count:
        values = [value + pltpu.roll(value, step, 0) for value in values]
        step //= 2
    while step:
        first = (line & step) == 0
        values = [
            jnp.where(first, a, b)
            + jnp.where(first, pltpu.roll(a, lines - step, 0), pltpu.roll(b, step, 0))
            for a, b in zip(values[:step], values[step:])
        ]
        step //= 2
    return values[0]


def multiply(ref, start, rows, tables_ref, which):
    values = ref[pl.ds(start, rows), :]
    high = values.astype(jnp.bfloat16)
    low = (values - high.astype(jnp.float32)).astype(jnp.bfloat16)
    dot = functools.partial(jnp.dot, preferred_element_type=jnp.float32)
    table_high = tables_ref[which]
    ref[pl.ds(start, rows), :] = (
        dot(high, table_high) + dot(low, table_high) + dot(high, tables_ref[which + 1])
    )


def team_sizes(sizes):
    return tuple(2 if size % 2 == 0 else 1 for size in sizes[:2])


def each(count, body):
    if count <= 32:
        for o in reversed(range(1, count)):
            body(o)
    else:
        pl.loop(1, count)(body)


def kernel(
    sizes,
    proj_hbm, first_hbm, bias_hbm, taps_hbm, second_hbm, cot_hbm, tables_hbm, turns_hbm, masks_hbm,
    sino_ref, first_out_ref, bias_out_ref, taps_out_ref, second_out_ref,
    proj_ref, first_vmem, bias_vmem, taps_ref, cot_ref, tables_ref, turns_ref, masks_ref,
    rows_ref, packed_ref, small_own,
    got, top, bottom, all_taps, all_packed, first_ref, second_ref,
    cot_shift, spec_back, spec_hidden, spec_taps, work,
    back, hidden_ref, gate_ref, filt, partial, mixed, lines_ref, first_matrix, grads_ref,
    outgoing, incoming, spread, gathered,
    rows_send, rows_recv, edge_send, edge_recv, taps_send, taps_recv,
    packed_send, packed_recv, sum_send, sum_recv, gather_send, gather_recv, load_sem, local_sem,
):
    ang_n, row_n, ch_n = sizes
    n = ang_n * row_n * ch_n
    angles, rq, columns = cot_ref.shape
    chans = second_ref.shape[2]
    chans_dev = taps_ref.shape[0]
    held = proj_ref.shape[0]
    both = angles * rq
    half = both // 2
    outer = columns // LANES
    block = outer * half
    depth = lines_ref.shape[0] // 2
    rp = depth // (3 * angles)
    team_n = incoming.shape[0]
    team_z, team_k = team_sizes(sizes)
    per = outer // team_n
    slab = lax.axis_index("slab")
    z, k, c0 = lax.axis_index("ang"), lax.axis_index("row"), lax.axis_index("ch")
    me = (z * row_n + k) * ch_n + c0

    paired = all(size & (size - 1) == 0 for size in sizes)

    def other(at, o, size):
        return at ^ o if paired else (at + o) % size

    def origin_of(at, o, size):
        return at ^ o if paired else (at + size - o) % size

    def partner(o):
        oz, ok, oc = o // (row_n * ch_n), o // ch_n % row_n, o % ch_n
        return other(z, oz, ang_n), other(k, ok, row_n), other(c0, oc, ch_n)

    def number(at):
        return (at[0] * row_n + at[1]) * ch_n + at[2]

    barrier = pltpu.get_barrier_semaphore()
    loads = [
        pltpu.make_async_copy(source, target, load_sem.at[at])
        for at, (source, target) in enumerate((
            (proj_hbm, proj_ref), (first_hbm, first_vmem), (bias_hbm, bias_vmem),
            (taps_hbm, taps_ref), (cot_hbm, cot_ref), (tables_hbm, tables_ref),
            (turns_hbm, turns_ref), (second_hbm, second_ref),
            (masks_hbm, masks_ref)))
    ]
    loads[0].start()
    each(n, lambda o: pl.semaphore_signal(
        barrier, inc=1, device_id=(slab, *partner(o)), device_id_type=MESH))
    for load in loads[1:]:
        load.start()

    def cols(m):
        return slice(m * LANES, (m + 1) * LANES)

    edge = jnp.zeros((outer, LANES), jnp.float32)
    rows_ref[0:outer, :] = edge
    rows_ref[(held + 1) * outer : (held + 2) * outer, :] = edge
    packed_ref[...] = jnp.zeros(packed_ref.shape, jnp.float32)
    loads[0].wait()
    for at in range(0, held, 8):
        for m in range(outer):
            rows_ref[pl.ds((at + 1) * outer + m, 8, stride=outer), :] = proj_ref[at : at + 8, cols(m)]
    loads[1].wait()
    loads[2].wait()
    for i in range(3):
        packed_ref[:, 3 * i : 3 * i + 3] = first_vmem[i]
    for l in range(chans_dev):
        packed_ref[l : l + 1, 9:10] = bias_vmem[0:1, l : l + 1]
    loads[3].wait()
    pl.semaphore_wait(barrier, n - 1)

    def all_of(source, target, send_sem, recv_sem):
        return pltpu.make_async_remote_copy(
            src_ref=source, dst_ref=target, send_sem=send_sem, recv_sem=recv_sem,
            device_id=(slab, *partner(1)), device_id_type=MESH)

    def rows_copy(o, slot, target):
        start = pl.multiple_of((target * ch_n + c0) * rq * outer, outer)
        return pltpu.make_async_remote_copy(
            src_ref=rows_ref.at[pl.ds(start, (rq + 2) * outer)], dst_ref=got.at[slot, pl.ds(0, (rq + 2) * outer)],
            send_sem=rows_send, recv_sem=rows_recv.at[slot],
            device_id=(slab, target, k, c0), device_id_type=MESH)

    def taps_copy(o, slot, target):
        return pltpu.make_async_remote_copy(
            src_ref=taps_ref, dst_ref=all_taps.at[slot],
            send_sem=taps_send, recv_sem=taps_recv,
            device_id=(slab, z, k, target), device_id_type=MESH)

    def packed_copy(o, slot, target):
        return pltpu.make_async_remote_copy(
            src_ref=packed_ref, dst_ref=all_packed.at[slot],
            send_sem=packed_send, recv_sem=packed_recv,
            device_id=(slab, z, k, target), device_id_type=MESH)

    def top_copy(slot):
        return pltpu.make_async_remote_copy(
            src_ref=rows_ref.at[pl.ds(held * outer, outer)], dst_ref=top.at[slot],
            send_sem=edge_send.at[0], recv_sem=edge_recv.at[0],
            device_id=(slab, 0, (k + 1) % row_n, 0), device_id_type=MESH)

    def bottom_copy(slot):
        return pltpu.make_async_remote_copy(
            src_ref=rows_ref.at[pl.ds(outer, outer)], dst_ref=bottom.at[slot],
            send_sem=edge_send.at[1], recv_sem=edge_recv.at[1],
            device_id=(slab, ang_n - 1, (k + row_n - 1) % row_n, ch_n - 1), device_id_type=MESH)

    for o in reversed(range(1, ang_n)):
        rows_copy(o, z, other(z, o, ang_n)).start()
    for o in range(1, ch_n):
        taps_copy(o, c0, (c0 + o) % ch_n).start()
        packed_copy(o, c0, (c0 + o) % ch_n).start()
    sends_top = jnp.logical_and(c0 == 0, k < row_n - 1)
    sends_bottom = jnp.logical_and(c0 == ch_n - 1, k > 0)

    @pl.when(sends_top)
    def _():
        top_copy(z).start()

    @pl.when(sends_bottom)
    def _():
        bottom_copy(z).start()

    mine_at = pl.multiple_of((z * ch_n + c0) * rq * outer, outer)
    for a in range(ang_n):
        got[a, (rq + 2) * outer : (rq + 3) * outer, :] = jnp.ones((outer, LANES), jnp.float32)
        if rp > rq + 3:
            rest = (rp - rq - 3) * outer
            got[a, (rq + 3) * outer : rp * outer, :] = jnp.zeros((rest, LANES), jnp.float32)
    got[z, 0 : (rq + 2) * outer, :] = rows_ref[pl.ds(mine_at, (rq + 2) * outer), :]
    all_taps[c0] = taps_ref[...]
    all_packed[c0] = packed_ref[...]

    def from_left(x):
        column = lax.broadcasted_iota(jnp.int32, x.shape, 1)
        return jnp.where(column == 0, 0.0, pltpu.roll(x, 1, 1))

    def from_right(x):
        column = lax.broadcasted_iota(jnp.int32, x.shape, 1)
        return jnp.where(column == columns - 1, 0.0, pltpu.roll(x, columns - 1, 1))

    lo, hi = slice(0, half), slice(half, both)
    re_l, im_l = slice(0, LANES), slice(LANES, 2 * LANES)

    loads[4].wait()
    upstream = jnp.concatenate([cot_ref[a] for a in range(angles)], axis=0)
    for i in range(3):
        shift = (i - 1) * rq % both
        turned = pltpu.roll(upstream, shift, 0) if shift else upstream
        cot_shift[3 * i] = from_right(turned)
        cot_shift[3 * i + 1] = turned
        cot_shift[3 * i + 2] = from_left(turned)

    def store_forward(ref, start, values):
        for q, (re, im) in enumerate(short_dft(values, -1)):
            part = slice(q * half, (q + 1) * half)
            cos, sin = turns_ref[0, part, :], turns_ref[1, part, :]
            rows = pl.ds(start + q * half, half)
            ref[rows, re_l] = re * cos + im * sin if q else re
            ref[rows, im_l] = im * cos - re * sin if q else im

    def load_inverse(ref, start):
        values = []
        for q in range(outer):
            part = slice(q * half, (q + 1) * half)
            cos, sin = turns_ref[0, part, :], turns_ref[1, part, :]
            rows = pl.ds(start + q * half, half)
            re, im = ref[rows, re_l], ref[rows, im_l]
            values.append((re * cos - im * sin, im * cos + re * sin) if q else (re, im))
        return short_dft(values, 1)

    def start_of(c):
        return pl.multiple_of(c * block, block)

    loads[5].wait()
    loads[6].wait()
    loads[7].wait()

    @pl.loop(0, chans)
    def _(c):
        weights = [second_ref[t // 3, t % 3, c] for t in range(9)]
        values = []
        for m in range(outer):
            pair = []
            for rows in (lo, hi):
                total = weights[0] * cot_shift[0, rows, cols(m)]
                for t in range(1, 9):
                    total = total + weights[t] * cot_shift[t, rows, cols(m)]
                pair.append(total)
            values.append(tuple(pair))
        store_forward(spec_back, start_of(c), values)

    step = 4 * block
    for s in range(0, chans * block, step):
        multiply(spec_back, s, step, tables_ref, 0)

    if ch_n > 1:
        all_of(all_taps.at[pl.ds(0, ch_n - 1)], all_taps.at[pl.ds(0, ch_n - 1)], taps_send, taps_recv).wait_recv()
        all_of(all_packed.at[pl.ds(0, ch_n - 1)], all_packed.at[pl.ds(0, ch_n - 1)], packed_send, packed_recv).wait_recv()
    load_weights = pltpu.make_async_copy(all_packed, first_ref, local_sem)
    load_weights.start()
    taps = jnp.concatenate([all_taps[h] for h in range(ch_n)], axis=0)
    zero = jnp.zeros((chans, LANES), jnp.float32)
    store_forward(spec_taps, 0, [(taps[:, cols(m)], zero) for m in range(outer)])
    multiply(spec_taps, 0, block, tables_ref, 0)

    def tap_row(q, c):
        row = spec_taps[pl.ds(q * half + c, 1), :]
        row = jnp.broadcast_to(row, (half, 2 * LANES))
        return row[:, re_l], row[:, im_l]

    @pl.loop(0, chans)
    def _(c):
        for q in range(outer):
            tr, ti = tap_row(q, c)
            rows = pl.ds(start_of(c) + q * half, half)
            gr, gi = spec_back[rows, re_l], spec_back[rows, im_l]
            work[rows, re_l] = tr * gr - ti * gi
            work[rows, im_l] = tr * gi + ti * gr

    for s in range(0, chans * block, step):
        multiply(work, s, step, tables_ref, 2)

    @pl.loop(0, chans)
    def _(c):
        for m, (re, im) in enumerate(load_inverse(work, start_of(c))):
            back[c, lo, cols(m)] = re
            back[c, hi, cols(m)] = im

    load_weights.wait()
    loads[8].wait()
    for c in range(0, chans, 2):
        totals = []
        for e in (c, c + 1):
            h, l = e // chans_dev, e % chans_dev
            total = first_ref[h, l, 9] * masks_ref[9]
            for t in range(9):
                total = total + first_ref[h, l, t] * masks_ref[t]
            totals.append(total)
        for side, rows in enumerate((lo, hi)):
            total = jnp.concatenate([value[rows, 0:depth] for value in totals], axis=0)
            high = total.astype(jnp.bfloat16)
            low = (total - high.astype(jnp.float32)) * masks_ref[10, :, 0:depth]
            first_matrix[side, c * half : (c + 2) * half, :] = high
            first_matrix[side, (chans + c) * half : (chans + c + 2) * half, :] = low.astype(jnp.bfloat16)

    has_top = jnp.logical_and(jnp.logical_and(z == 0, c0 == 0), k > 0)
    has_bottom = jnp.logical_and(jnp.logical_and(z == ang_n - 1, c0 == ch_n - 1), k < row_n - 1)

    @pl.when(has_top)
    def _():
        all_of(top, top, edge_send.at[0], edge_recv.at[0]).wait_recv()

    @pl.when(has_bottom)
    def _():
        all_of(bottom, bottom, edge_send.at[1], edge_recv.at[1]).wait_recv()

    def prepare(a):
        @pl.when(has_top)
        def _():
            got[a, 0:outer, :] = top[a]

        @pl.when(has_bottom)
        def _():
            got[a, (rq + 1) * outer : (rq + 2) * outer, :] = bottom[a]

        centre = jnp.concatenate(
            [got[a, pl.ds(m, rp, stride=outer), :] for m in range(outer)], axis=1)
        lines = jnp.concatenate([from_left(centre), centre, from_right(centre)], axis=0)
        high = lines.astype(jnp.bfloat16).astype(jnp.float32)
        at = pl.multiple_of(a * 6 * rp, 6 * rp)
        lines_ref[pl.ds(at, 6 * rp), :] = jnp.concatenate(
            [high, lines - high], axis=0).astype(jnp.bfloat16)

    dot = functools.partial(jnp.dot, preferred_element_type=jnp.float32)

    def activate(side):
        at = pl.ds(pl.multiple_of(side * chans * half, chans * half), chans * half)
        rows = pl.ds(pl.multiple_of(side * depth, depth), depth)
        for start in range(0, columns, 2 * LANES):
            chunk = slice(start, start + 2 * LANES)
            total = dot(first_matrix[side], lines_ref[rows, chunk])
            total = total[0 : chans * half] + total[chans * half : 2 * chans * half]
            gate = 0.5 + 0.5 * jnp.tanh(0.5 * total)
            gate_ref[at, chunk] = gate
            hidden_ref[at, chunk] = total * gate

    near_n = ang_n // 2
    near = z // near_n
    prepare(z)
    for side, first in ((near, 1), (1 - near, 0)):
        for o in range(first, near_n):
            origin = side * near_n + (z % near_n + o) % near_n
            rows_copy(o, origin, origin).wait_recv()
            prepare(origin)
        activate(side)

    group = chans // 2
    line_of = lax.broadcasted_iota(jnp.int32, (half, LANES), 0)

    def cross(first):
        for q in range(outer):
            at = slice(chans * block + q * half, chans * block + (q + 1) * half)
            reals, imags = [], []
            for c in range(first, first + group):
                line = slice(c * block + q * half, c * block + (q + 1) * half)
                gr, gi = spec_back[line, re_l], spec_back[line, im_l]
                hr, hi_ = spec_hidden[line, re_l], spec_hidden[line, im_l]
                reals.append(gr * hr + gi * hi_)
                imags.append(gr * hi_ - gi * hr)
            for side, values in ((re_l, reals), (im_l, imags)):
                value = fold_rows(values)
                work[at, side] = value if first == 0 else jnp.where(line_of < group, work[at, side], value)

    for c in range(chans):
        values = [
            (hidden_ref[c * half : (c + 1) * half, cols(m)],
             hidden_ref[(chans + c) * half : (chans + c + 1) * half, cols(m)])
            for m in range(outer)]
        store_forward(spec_hidden, c * block, values)
        if c + 1 == group:
            multiply(spec_hidden, 0, group * block, tables_ref, 0)
    cross(0)
    multiply(spec_hidden, group * block, group * block, tables_ref, 0)
    cross(group)

    multiply(work, chans * block, block, tables_ref, 2)
    for m, (re, im) in enumerate(load_inverse(work, chans * block)):
        outgoing[m] = re

    def folded(value):
        return jnp.sum(value, axis=0, keepdims=True)

    def mate(o):
        oz, ok, oc = o // (team_k * ch_n), o // ch_n % team_k, o % ch_n
        there_z = z // team_z * team_z + (z + oz) % team_z
        there_k = k // team_k * team_k + (k + ok) % team_k
        return there_z, there_k, (c0 + oc) % ch_n

    def rank(at):
        return (at[0] % team_z * team_k + at[1] % team_k) * ch_n + at[2]

    def sum_copy(o):
        target = mate(o)
        return pltpu.make_async_remote_copy(
            src_ref=outgoing.at[pl.ds(rank(target) * per, per)], dst_ref=incoming.at[o],
            send_sem=sum_send, recv_sem=sum_recv,
            device_id=(slab, *target), device_id_type=MESH)

    each(team_n, lambda o: sum_copy(o).start())

    @pl.loop(0, chans)
    def _(c):
        for q in range(outer):
            tr, ti = tap_row(q, c)
            rows = pl.ds(start_of(c) + q * half, half)
            hr, hi_ = spec_hidden[rows, re_l], spec_hidden[rows, im_l]
            work[rows, re_l] = tr * hr + ti * hi_
            work[rows, im_l] = tr * hi_ - ti * hr

    for s in range(0, chans * block, step):
        multiply(work, s, step, tables_ref, 2)

    partial[...] = jnp.zeros(partial.shape, jnp.float32)

    @pl.loop(0, chans // 2)
    def _(c):
        for side, rows in enumerate((lo, hi)):
            at = pl.ds(pl.multiple_of(side * chans * half + c * both, both), both)
            at_high = pl.ds(pl.multiple_of(c * both, both), both)
            at_low = pl.ds(pl.multiple_of(chans * half + c * both, both), both)
            for m in range(outer):
                gate = gate_ref[at, cols(m)]
                grad = jnp.concatenate([back[2 * c, rows, cols(m)], back[2 * c + 1, rows, cols(m)]], axis=0)
                grad = grad * (gate + hidden_ref[at, cols(m)] * (1.0 - gate))
                high = grad.astype(jnp.bfloat16)
                grads_ref[side, at_high, cols(m)] = high
                grads_ref[side, at_low, cols(m)] = (grad - high.astype(jnp.float32)).astype(jnp.bfloat16)

    wide = masks_ref.shape[2]
    totals = []
    for side in range(2):
        total = lax.dot_general(
            grads_ref[side], lines_ref[side * depth : (side + 1) * depth, :], (((1,), (1,)), ((), ())),
            preferred_element_type=jnp.float32)
        total = total[0 : chans * half] + total[chans * half : 2 * chans * half]
        if wide > depth:
            total = jnp.concatenate([total, jnp.zeros((chans * half, wide - depth), jnp.float32)], axis=1)
        totals.append(total)
    for c in range(chans):
        values = []
        for t in range(10):
            value = totals[0][c * half : (c + 1) * half] * masks_ref[t, lo, :]
            value = value + totals[1][c * half : (c + 1) * half] * masks_ref[t, hi, :]
            values.append(functools.reduce(
                lambda x, y: x + y, [value[:, at : at + LANES] for at in range(0, wide, LANES)]))
        partial[c, 0:8, :] = fold_rows(values[0:8])
        partial[c, 8:9, :] = folded(values[8])
        partial[c, 9:10, :] = folded(values[9])

    @pl.loop(0, chans)
    def _(c):
        sums = [jnp.zeros((half, LANES), jnp.float32) for _ in range(9)]
        for m, (re, im) in enumerate(load_inverse(work, start_of(c))):
            filt[c, lo, cols(m)] = re
            filt[c, hi, cols(m)] = im
            for t in range(9):
                sums[t] = sums[t] + re * cot_shift[t, lo, cols(m)] + im * cot_shift[t, hi, cols(m)]
        for t in range(9):
            partial[c, 16 + t : 17 + t, :] = folded(sums[t])

    small = lax.dot_general(
        jnp.ones((8, LANES), jnp.float32), partial[...].reshape(chans * SLOTS, LANES),
        (((1,), (1,)), ((), ())),
        precision=lax.Precision.HIGHEST, preferred_element_type=jnp.float32)
    width = chans_dev * SLOTS
    for h in range(ch_n):
        small_own[h] = small[0:1, h * width : (h + 1) * width]

    mine = pl.multiple_of(rank((z, k, c0)) * per, per)
    total = outgoing[pl.ds(mine, per)]
    summed = incoming.at[pl.ds(1, team_n - 1)]
    all_of(summed, summed, sum_send, sum_recv).wait_recv()
    for o in range(1, team_n):
        total = total + incoming[o]
    used = per * chans_dev
    for h in range(ch_n):
        for p in range(per):
            at = slice(p * chans_dev, (p + 1) * chans_dev)
            spread[h, at, :] = total[p, h * chans_dev : (h + 1) * chans_dev]
        spread[h, used : used + 1, :] = small_own[h]
    spreads = gathered.at[pl.ds(0, n - 1), pl.ds(0, used + 1)]

    def gather_copy(o):
        target = partner(o)
        return pltpu.make_async_remote_copy(
            src_ref=spread.at[target[2], pl.ds(0, used + 1)], dst_ref=gathered.at[me, pl.ds(0, used + 1)],
            send_sem=gather_send, recv_sem=gather_recv,
            device_id=(slab, *target), device_id_type=MESH)

    each(n, lambda o: gather_copy(o).start())
    gathered[me] = spread[c0]

    @pl.loop(0, outer)
    def _(m):
        at = pl.ds(pl.multiple_of(m * LANES, LANES), LANES)
        for rows in (lo, hi):
            pieces = [filt[c, rows, at] for c in range(chans)]
            for t in range(9):
                total = second_ref[t // 3, t % 3, 0] * pieces[0]
                for c in range(1, chans):
                    total = total + second_ref[t // 3, t % 3, c] * pieces[c]
                mixed[t, rows, at] = total

    sides = []
    for j in range(3):
        total = mixed[3 + j]
        for i in (0, 2):
            total = total + pltpu.roll(mixed[3 * i + j], -(i - 1) * rq % both, 0)
        sides.append(total)
    image = sides[1] + from_left(sides[0]) + from_right(sides[2])
    for a in range(angles):
        sino_ref[a] = image[a * rq : (a + 1) * rq]

    if ang_n > 1:
        sent = got.at[pl.ds(0, ang_n - 1), pl.ds(0, (rq + 2) * outer)]
        all_of(sent, sent, rows_send, rows_recv.at[0]).wait_send()
    if ch_n > 1:
        sent = all_taps.at[pl.ds(0, ch_n - 1)]
        all_of(sent, sent, taps_send, taps_recv).wait_send()
        sent = all_packed.at[pl.ds(0, ch_n - 1)]
        all_of(sent, sent, packed_send, packed_recv).wait_send()

    @pl.when(sends_top)
    def _():
        top_copy(z).wait_send()

    @pl.when(sends_bottom)
    def _():
        bottom_copy(z).wait_send()

    all_of(summed, summed, sum_send, sum_recv).wait_send()

    all_of(spreads, spreads, gather_send, gather_recv).wait_recv()
    sums = gathered[0, used : used + 1, :]
    for d in range(1, n):
        sums = sums + gathered[d, used : used + 1, :]
    for l in range(chans_dev):
        for i in range(3):
            at = l * SLOTS + 3 * i
            first_out_ref[i, l : l + 1, :] = sums[:, at : at + 3]
            second_out_ref[i, l : l + 1, :] = sums[:, at + 16 : at + 19]
        bias_out_ref[0:1, l : l + 1] = sums[:, l * SLOTS + 9 : l * SLOTS + 10]

    for m in range(outer):
        owner, at = m // per, m % per
        rz, rk, rc = owner // (team_k * ch_n), owner // ch_n % team_k, owner % ch_n
        pieces = [
            gathered[number((jz + rz, jk + rk, rc)), at * chans_dev : (at + 1) * chans_dev, :]
            for jz in range(0, ang_n, team_z) for jk in range(0, row_n, team_k)]
        taps_out_ref[:, cols(m)] = functools.reduce(lambda x, y: x + y, pieces)

    all_of(spreads, spreads, gather_send, gather_recv).wait_send()


def deliver(*refs):
    count = (len(refs) - 1) // 2
    sources, targets, sems = refs[:count], refs[count : 2 * count], refs[-1]
    copies = [pltpu.make_async_copy(sources[at], targets[at], sems.at[at]) for at in range(count)]
    for copy in copies:
        copy.start()
    for copy in copies:
        copy.wait()


def on_device(sizes, tables, projections, conv1_weight, conv1_bias, filter_taps, conv2_weight, cotangent):
    ang_n, row_n, ch_n = sizes
    n = ang_n * row_n * ch_n
    _, held, columns = projections.shape
    chans_dev = conv1_weight.shape[0]
    chans = chans_dev * ch_n
    _, angles, rq, _ = cotangent.shape
    outer = columns // LANES
    both = angles * rq
    block = outer * both // 2
    rp = padded_rows(rq)
    team_n = math.prod(team_sizes(sizes)) * ch_n
    slot = -(-(outer // team_n * chans_dev + 1) // 8) * 8
    f32 = jnp.float32
    vmem = pl.BlockSpec(memory_space=pltpu.VMEM)
    hbm = pl.BlockSpec(memory_space=pltpu.HBM)
    dma = pltpu.SemaphoreType.DMA
    wide = (both, columns)
    shapes = (
        jax.ShapeDtypeStruct((angles, rq, columns), f32),
        jax.ShapeDtypeStruct((3, chans_dev, 3), f32),
        jax.ShapeDtypeStruct((1, chans_dev), f32),
        jax.ShapeDtypeStruct((chans_dev, columns), f32),
        jax.ShapeDtypeStruct((3, chans_dev, 3), f32),
    )
    results = pl.pallas_call(
        functools.partial(kernel, sizes),
        out_shape=tuple(pltpu.VMEM(leaf.shape, f32) for leaf in shapes),
        in_specs=[hbm] * 9,
        out_specs=(vmem,) * 5,
        scratch_shapes=[
            pltpu.VMEM((held, columns), f32),
            pltpu.VMEM((3, chans_dev, 3), f32),
            pltpu.VMEM((1, chans_dev), f32),
            pltpu.VMEM((chans_dev, columns), f32),
            pltpu.VMEM((angles, rq, columns), f32),
            pltpu.VMEM(tables[0].shape, jnp.bfloat16),
            pltpu.VMEM(tables[1].shape, f32),
            pltpu.VMEM(tables[2].shape, f32),
            pltpu.VMEM(((held + 2) * outer, LANES), f32),
            pltpu.VMEM((chans_dev, LANES), f32),
            pltpu.VMEM((ch_n, 1, LANES), f32),
            pltpu.VMEM((ang_n, rp * outer, LANES), f32),
            pltpu.VMEM((ang_n, outer, LANES), f32),
            pltpu.VMEM((ang_n, outer, LANES), f32),
            pltpu.VMEM((ch_n, chans_dev, columns), f32),
            pltpu.VMEM((ch_n, chans_dev, LANES), f32),
            pltpu.SMEM((ch_n, chans_dev, LANES), f32),
            pltpu.SMEM((3, 3, chans), f32),
            pltpu.VMEM((9,) + wide, f32),
            pltpu.VMEM((chans * block, 2 * LANES), f32),
            pltpu.VMEM((chans * block, 2 * LANES), f32),
            pltpu.VMEM((block, 2 * LANES), f32),
            pltpu.VMEM(((chans + 1) * block, 2 * LANES), f32),
            pltpu.VMEM((chans,) + wide, f32),
            pltpu.VMEM((chans * both, columns), f32),
            pltpu.VMEM((chans * both, columns), f32),
            pltpu.VMEM((chans,) + wide, f32),
            pltpu.VMEM((chans, SLOTS, LANES), f32),
            pltpu.VMEM((9,) + wide, f32),
            pltpu.VMEM((angles * 6 * rp, columns), jnp.bfloat16),
            pltpu.VMEM((2, chans * both, angles * 3 * rp), jnp.bfloat16),
            pltpu.VMEM((2, chans * both, columns), jnp.bfloat16),
            pltpu.VMEM((outer, chans, LANES), f32),
            pltpu.VMEM((team_n, outer // team_n, chans, LANES), f32),
            pltpu.VMEM((ch_n, slot, LANES), f32),
            pltpu.VMEM((n, slot, LANES), f32),
            dma(()), dma((ang_n,)), dma((2,)), dma((2,)),
            dma(()), dma(()), dma(()), dma(()),
            dma(()), dma(()), dma(()), dma(()), dma((9,)), dma(()),
        ],
        compiler_params=pltpu.CompilerParams(
            collective_id=0, has_side_effects=True, vmem_limit_bytes=63 * 2**20
        ),
        name="tomography",
    )(
        projections[0], jnp.transpose(conv1_weight, (1, 0, 2)), conv1_bias[None], filter_taps,
        jnp.transpose(conv2_weight, (1, 2, 0)), cotangent[0], *tables,
    )
    image, first, bias, taps_out, second = pl.pallas_call(
        deliver,
        out_shape=shapes,
        in_specs=[vmem] * 5,
        out_specs=(hbm,) * 5,
        scratch_shapes=[dma((5,))],
        name="deliver",
    )(*[pltpu.with_memory_space_constraint(leaf, pltpu.VMEM) for leaf in results])
    return (
        image[None], jnp.transpose(first, (1, 0, 2)), bias[0], taps_out,
        jnp.transpose(second, (1, 0, 2)),
    )


def solution(mesh):
    sizes = tuple(mesh.shape[axis] for axis in ("ang", "row", "ch"))

    def whole(projections, conv1_weight, conv1_bias, filter_taps, conv2_weight, cotangent):
        angles, rq = cotangent.shape[1], cotangent.shape[2] // (sizes[0] * sizes[2])
        tables = (*make_tables(projections.shape[-1]), make_masks(angles, rq))

        def local(*arrays):
            return on_device(sizes, tuple(jnp.asarray(t) for t in tables), *arrays)

        return jax.shard_map(
            local,
            mesh=mesh,
            in_specs=(
                P(("slab", "ang"), "row", None),
                P("ch", None, None),
                P("ch"),
                P("ch", None),
                P(),
                P(("slab", "row"), None, ("ang", "ch"), None),
            ),
            out_specs=(
                P(("slab", "row"), None, ("ang", "ch"), None),
                P(("slab", "ch"), None, None),
                P(("slab", "ch")),
                P(("slab", "ch"), None),
                P(("slab", "ch"), None, None),
            ),
            check_vma=False,
        )(projections, conv1_weight, conv1_bias, filter_taps, conv2_weight, cotangent)

    return whole
```

```python
import functools
import math

import jax
import jax.numpy as jnp
import numpy as np
import ml_dtypes
from jax import lax
from jax.experimental import pallas as pl
from jax.experimental.pallas import tpu as pltpu
from jax.sharding import PartitionSpec as P

MESH = pl.DeviceIdType.MESH
LANES = 128
SLOTS = 32


def twisted(value, k, n, sign):
    re, im = value
    if k == 0:
        return value
    if 4 * k == n:
        return (-im, re) if sign > 0 else (im, -re)
    if 8 * k == n:
        half = math.sqrt(0.5)
        return (half * (re - sign * im), half * (im + sign * re))
    if 8 * k == 3 * n:
        half = math.sqrt(0.5)
        return (half * (-re - sign * im), half * (-im + sign * re))
    cos = math.cos(2 * math.pi * k / n)
    sin = sign * math.sin(2 * math.pi * k / n)
    return (cos * re - sin * im, cos * im + sin * re)


def short_dft(values, sign):
    n = len(values)
    if n == 1:
        return values
    even = short_dft(values[0::2], sign)
    odd = short_dft(values[1::2], sign)
    low, high = [], []
    for k in range(n // 2):
        re, im = twisted(odd[k], k, n, sign)
        low.append((even[k][0] + re, even[k][1] + im))
        high.append((even[k][0] - re, even[k][1] - im))
    return low + high


def split_high_low(table):
    high = table.astype(ml_dtypes.bfloat16)
    low = (table - high.astype(np.float64)).astype(ml_dtypes.bfloat16)
    return high, low


def make_tables(length):
    outer = length // LANES
    index = np.arange(LANES)
    inner = 2 * np.pi * (np.outer(index, index) % LANES) / LANES
    cos, sin = np.cos(inner), np.sin(inner)
    forward = np.block([[cos, -sin], [sin, cos]])
    inverse = np.block([[cos, sin], [-sin, cos]]) / length
    twist = 2 * np.pi * np.outer(np.arange(outer), index) / length
    twist = np.repeat(twist, 8, axis=0)
    tables = np.stack([*split_high_low(forward), *split_high_low(inverse)])
    turns = np.stack([np.cos(twist), np.sin(twist)]).astype(np.float32)
    return tables, turns


def padded_rows(rq):
    return -(-(rq + 3) // 8) * 8


def make_masks(angles, rq):
    rp = padded_rows(rq)
    near = angles // 2
    masks = np.zeros((11, angles, rq, near, 2, 3, rp), np.float32)
    for a in range(angles):
        for r in range(rq):
            for t in range(9):
                masks[t, a, r, a % near, :, t % 3, r + t // 3] = 1
            masks[9, a, r, a % near, 0, 1, rq + 2] = 1
            masks[10, a, r, :, 0] = 1
    masks = masks.reshape(11, angles * rq, near * 6 * rp)
    return np.pad(masks, ((0, 0), (0, 0), (0, -masks.shape[2] % LANES)))


def fold_rows(values):
    count, lines = len(values), values[0].shape[0]
    line = lax.broadcasted_iota(jnp.int32, values[0].shape, 0)
    step = lines // 2
    while step >= count:
        values = [value + pltpu.roll(value, step, 0) for value in values]
        step //= 2
    while step:
        first = (line & step) == 0
        values = [
            jnp.where(first, a, b)
            + jnp.where(first, pltpu.roll(a, lines - step, 0), pltpu.roll(b, step, 0))
            for a, b in zip(values[:step], values[step:])
        ]
        step //= 2
    return values[0]


def multiply(ref, start, rows, tables_ref, which):
    values = ref[pl.ds(start, rows), :]
    high = values.astype(jnp.bfloat16)
    low = (values - high.astype(jnp.float32)).astype(jnp.bfloat16)
    dot = functools.partial(jnp.dot, preferred_element_type=jnp.float32)
    table_high = tables_ref[which]
    ref[pl.ds(start, rows), :] = (
        dot(high, table_high) + dot(low, table_high) + dot(high, tables_ref[which + 1])
    )


def team_sizes(sizes):
    return tuple(2 if size % 2 == 0 else 1 for size in sizes[:2])


def each(count, body):
    if count <= 32:
        for o in reversed(range(1, count)):
            body(o)
    else:
        pl.loop(1, count)(body)


def kernel(
    sizes,
    proj_hbm, first_hbm, bias_hbm, taps_hbm, second_hbm, cot_hbm, tables_hbm, turns_hbm, masks_hbm,
    sino_ref, first_out_ref, bias_out_ref, taps_out_ref, second_out_ref,
    proj_ref, first_vmem, bias_vmem, taps_ref, cot_ref, tables_ref, turns_ref, masks_ref,
    rows_ref, packed_ref, small_own,
    got, top, bottom, all_taps, all_packed, first_ref, second_ref,
    cot_shift, spec_back, spec_hidden, spec_taps, work,
    back, hidden_ref, gate_ref, filt, partial, mixed, lines_ref, first_matrix, grads_ref,
    outgoing, incoming, spread, gathered,
    rows_send, rows_recv, edge_send, edge_recv, taps_send, taps_recv,
    packed_send, packed_recv, sum_send, sum_recv, gather_send, gather_recv, load_sem, local_sem,
):
    ang_n, row_n, ch_n = sizes
    n = ang_n * row_n * ch_n
    angles, rq, columns = cot_ref.shape
    chans = second_ref.shape[2]
    chans_dev = taps_ref.shape[0]
    held = proj_ref.shape[0]
    both = angles * rq
    half = both // 2
    outer = columns // LANES
    block = outer * half
    depth = lines_ref.shape[0] // 2
    rp = depth // (3 * angles)
    team_n = incoming.shape[0]
    team_z, team_k = team_sizes(sizes)
    per = outer // team_n
    slab = lax.axis_index("slab")
    z, k, c0 = lax.axis_index("ang"), lax.axis_index("row"), lax.axis_index("ch")
    me = (z * row_n + k) * ch_n + c0

    paired = all(size & (size - 1) == 0 for size in sizes)

    def other(at, o, size):
        return at ^ o if paired else (at + o) % size

    def origin_of(at, o, size):
        return at ^ o if paired else (at + size - o) % size

    def partner(o):
        oz, ok, oc = o // (row_n * ch_n), o // ch_n % row_n, o % ch_n
        return other(z, oz, ang_n), other(k, ok, row_n), other(c0, oc, ch_n)

    def number(at):
        return (at[0] * row_n + at[1]) * ch_n + at[2]

    barrier = pltpu.get_barrier_semaphore()
    loads = [
        pltpu.make_async_copy(source, target, load_sem.at[at])
        for at, (source, target) in enumerate((
            (proj_hbm, proj_ref), (first_hbm, first_vmem), (bias_hbm, bias_vmem),
            (taps_hbm, taps_ref), (cot_hbm, cot_ref), (tables_hbm, tables_ref),
            (turns_hbm, turns_ref), (second_hbm, second_ref),
            (masks_hbm, masks_ref)))
    ]
    loads[0].start()
    each(n, lambda o: pl.semaphore_signal(
        barrier, inc=1, device_id=(slab, *partner(o)), device_id_type=MESH))
    for load in loads[1:]:
        load.start()

    def cols(m):
        return slice(m * LANES, (m + 1) * LANES)

    edge = jnp.zeros((outer, LANES), jnp.float32)
    rows_ref[0:outer, :] = edge
    rows_ref[(held + 1) * outer : (held + 2) * outer, :] = edge
    packed_ref[...] = jnp.zeros(packed_ref.shape, jnp.float32)
    loads[0].wait()
    for at in range(0, held, 8):
        for m in range(outer):
            rows_ref[pl.ds((at + 1) * outer + m, 8, stride=outer), :] = proj_ref[at : at + 8, cols(m)]
    pl.semaphore_wait(barrier, n - 1)

    def all_of(source, target, send_sem, recv_sem):
        return pltpu.make_async_remote_copy(
            src_ref=source, dst_ref=target, send_sem=send_sem, recv_sem=recv_sem,
            device_id=(slab, *partner(1)), device_id_type=MESH)

    def rows_copy(o, slot, target):
        start = pl.multiple_of((target * ch_n + c0) * rq * outer, outer)
        return pltpu.make_async_remote_copy(
            src_ref=rows_ref.at[pl.ds(start, (rq + 2) * outer)], dst_ref=got.at[slot, pl.ds(0, (rq + 2) * outer)],
            send_sem=rows_send, recv_sem=rows_recv.at[slot],
            device_id=(slab, target, k, c0), device_id_type=MESH)

    def taps_copy(o, slot, target):
        return pltpu.make_async_remote_copy(
            src_ref=taps_ref, dst_ref=all_taps.at[slot],
            send_sem=taps_send, recv_sem=taps_recv,
            device_id=(slab, z, k, target), device_id_type=MESH)

    def packed_copy(o, slot, target):
        return pltpu.make_async_remote_copy(
            src_ref=packed_ref, dst_ref=all_packed.at[slot],
            send_sem=packed_send, recv_sem=packed_recv,
            device_id=(slab, z, k, target), device_id_type=MESH)

    def top_copy(slot):
        return pltpu.make_async_remote_copy(
            src_ref=rows_ref.at[pl.ds(held * outer, outer)], dst_ref=top.at[slot],
            send_sem=edge_send.at[0], recv_sem=edge_recv.at[0],
            device_id=(slab, 0, (k + 1) % row_n, 0), device_id_type=MESH)

    def bottom_copy(slot):
        return pltpu.make_async_remote_copy(
            src_ref=rows_ref.at[pl.ds(outer, outer)], dst_ref=bottom.at[slot],
            send_sem=edge_send.at[1], recv_sem=edge_recv.at[1],
            device_id=(slab, ang_n - 1, (k + row_n - 1) % row_n, ch_n - 1), device_id_type=MESH)

    for o in reversed(range(1, ang_n)):
        rows_copy(o, z, other(z, o, ang_n)).start()
    sends_top = jnp.logical_and(c0 == 0, k < row_n - 1)
    sends_bottom = jnp.logical_and(c0 == ch_n - 1, k > 0)

    @pl.when(sends_top)
    def _():
        top_copy(z).start()

    @pl.when(sends_bottom)
    def _():
        bottom_copy(z).start()

    loads[1].wait()
    loads[2].wait()
    for i in range(3):
        packed_ref[:, 3 * i : 3 * i + 3] = first_vmem[i]
    for l in range(chans_dev):
        packed_ref[l : l + 1, 9:10] = bias_vmem[0:1, l : l + 1]
    loads[3].wait()
    for o in range(1, ch_n):
        taps_copy(o, c0, (c0 + o) % ch_n).start()
        packed_copy(o, c0, (c0 + o) % ch_n).start()
    mine_at = pl.multiple_of((z * ch_n + c0) * rq * outer, outer)
    for a in range(ang_n):
        got[a, (rq + 2) * outer : (rq + 3) * outer, :] = jnp.ones((outer, LANES), jnp.float32)
        if rp > rq + 3:
            rest = (rp - rq - 3) * outer
            got[a, (rq + 3) * outer : rp * outer, :] = jnp.zeros((rest, LANES), jnp.float32)
    got[z, 0 : (rq + 2) * outer, :] = rows_ref[pl.ds(mine_at, (rq + 2) * outer), :]
    all_taps[c0] = taps_ref[...]
    all_packed[c0] = packed_ref[...]

    def from_left(x):
        column = lax.broadcasted_iota(jnp.int32, x.shape, 1)
        return jnp.where(column == 0, 0.0, pltpu.roll(x, 1, 1))

    def from_right(x):
        column = lax.broadcasted_iota(jnp.int32, x.shape, 1)
        return jnp.where(column == columns - 1, 0.0, pltpu.roll(x, columns - 1, 1))

    lo, hi = slice(0, half), slice(half, both)
    re_l, im_l = slice(0, LANES), slice(LANES, 2 * LANES)

    loads[4].wait()
    upstream = jnp.concatenate([cot_ref[a] for a in range(angles)], axis=0)
    for i in range(3):
        shift = (i - 1) * rq % both
        turned = pltpu.roll(upstream, shift, 0) if shift else upstream
        cot_shift[3 * i] = from_right(turned)
        cot_shift[3 * i + 1] = turned
        cot_shift[3 * i + 2] = from_left(turned)

    def store_forward(ref, start, values):
        for q, (re, im) in enumerate(short_dft(values, -1)):
            part = slice(q * half, (q + 1) * half)
            cos, sin = turns_ref[0, part, :], turns_ref[1, part, :]
            rows = pl.ds(start + q * half, half)
            ref[rows, re_l] = re * cos + im * sin if q else re
            ref[rows, im_l] = im * cos - re * sin if q else im

    def load_inverse(ref, start):
        values = []
        for q in range(outer):
            part = slice(q * half, (q + 1) * half)
            cos, sin = turns_ref[0, part, :], turns_ref[1, part, :]
            rows = pl.ds(start + q * half, half)
            re, im = ref[rows, re_l], ref[rows, im_l]
            values.append((re * cos - im * sin, im * cos + re * sin) if q else (re, im))
        return short_dft(values, 1)

    def start_of(c):
        return pl.multiple_of(c * block, block)

    loads[5].wait()
    loads[6].wait()
    loads[7].wait()

    @pl.loop(0, chans)
    def _(c):
        weights = [second_ref[t // 3, t % 3, c] for t in range(9)]
        values = []
        for m in range(outer):
            pair = []
            for rows in (lo, hi):
                total = weights[0] * cot_shift[0, rows, cols(m)]
                for t in range(1, 9):
                    total = total + weights[t] * cot_shift[t, rows, cols(m)]
                pair.append(total)
            values.append(tuple(pair))
        store_forward(spec_back, start_of(c), values)

    step = 4 * block
    for s in range(0, chans * block, step):
        multiply(spec_back, s, step, tables_ref, 0)

    if ch_n > 1:
        all_of(all_taps.at[pl.ds(0, ch_n - 1)], all_taps.at[pl.ds(0, ch_n - 1)], taps_send, taps_recv).wait_recv()
        all_of(all_packed.at[pl.ds(0, ch_n - 1)], all_packed.at[pl.ds(0, ch_n - 1)], packed_send, packed_recv).wait_recv()
    load_weights = pltpu.make_async_copy(all_packed, first_ref, local_sem)
    load_weights.start()
    taps = jnp.concatenate([all_taps[h] for h in range(ch_n)], axis=0)
    zero = jnp.zeros((chans, LANES), jnp.float32)
    store_forward(spec_taps, 0, [(taps[:, cols(m)], zero) for m in range(outer)])
    multiply(spec_taps, 0, block, tables_ref, 0)

    def tap_row(q, c):
        row = spec_taps[pl.ds(q * half + c, 1), :]
        row = jnp.broadcast_to(row, (half, 2 * LANES))
        return row[:, re_l], row[:, im_l]

    @pl.loop(0, chans)
    def _(c):
        for q in range(outer):
            tr, ti = tap_row(q, c)
            rows = pl.ds(start_of(c) + q * half, half)
            gr, gi = spec_back[rows, re_l], spec_back[rows, im_l]
            work[rows, re_l] = tr * gr - ti * gi
            work[rows, im_l] = tr * gi + ti * gr

    for s in range(0, chans * block, step):
        multiply(work, s, step, tables_ref, 2)

    @pl.loop(0, chans)
    def _(c):
        for m, (re, im) in enumerate(load_inverse(work, start_of(c))):
            back[c, lo, cols(m)] = re
            back[c, hi, cols(m)] = im

    load_weights.wait()
    loads[8].wait()
    for c in range(0, chans, 2):
        totals = []
        for e in (c, c + 1):
            h, l = e // chans_dev, e % chans_dev
            total = first_ref[h, l, 9] * masks_ref[9]
            for t in range(9):
                total = total + first_ref[h, l, t] * masks_ref[t]
            totals.append(total)
        for side, rows in enumerate((lo, hi)):
            total = jnp.concatenate([value[rows, 0:depth] for value in totals], axis=0)
            high = total.astype(jnp.bfloat16)
            low = (total - high.astype(jnp.float32)) * masks_ref[10, :, 0:depth]
            first_matrix[side, c * half : (c + 2) * half, :] = high
            first_matrix[side, (chans + c) * half : (chans + c + 2) * half, :] = low.astype(jnp.bfloat16)

    has_top = jnp.logical_and(jnp.logical_and(z == 0, c0 == 0), k > 0)
    has_bottom = jnp.logical_and(jnp.logical_and(z == ang_n - 1, c0 == ch_n - 1), k < row_n - 1)

    @pl.when(has_top)
    def _():
        all_of(top, top, edge_send.at[0], edge_recv.at[0]).wait_recv()

    @pl.when(has_bottom)
    def _():
        all_of(bottom, bottom, edge_send.at[1], edge_recv.at[1]).wait_recv()

    def prepare(a):
        @pl.when(has_top)
        def _():
            got[a, 0:outer, :] = top[a]

        @pl.when(has_bottom)
        def _():
            got[a, (rq + 1) * outer : (rq + 2) * outer, :] = bottom[a]

        centre = jnp.concatenate(
            [got[a, pl.ds(m, rp, stride=outer), :] for m in range(outer)], axis=1)
        lines = jnp.concatenate([from_left(centre), centre, from_right(centre)], axis=0)
        high = lines.astype(jnp.bfloat16).astype(jnp.float32)
        at = pl.multiple_of(a * 6 * rp, 6 * rp)
        lines_ref[pl.ds(at, 6 * rp), :] = jnp.concatenate(
            [high, lines - high], axis=0).astype(jnp.bfloat16)

    dot = functools.partial(jnp.dot, preferred_element_type=jnp.float32)

    def activate(side):
        at = pl.ds(pl.multiple_of(side * chans * half, chans * half), chans * half)
        rows = pl.ds(pl.multiple_of(side * depth, depth), depth)
        for start in range(0, columns, 2 * LANES):
            chunk = slice(start, start + 2 * LANES)
            total = dot(first_matrix[side], lines_ref[rows, chunk])
            total = total[0 : chans * half] + total[chans * half : 2 * chans * half]
            gate = 0.5 + 0.5 * jnp.tanh(0.5 * total)
            gate_ref[at, chunk] = gate
            hidden_ref[at, chunk] = total * gate

    near_n = ang_n // 2
    near = z // near_n
    prepare(z)
    for side, first in ((near, 1), (1 - near, 0)):
        for o in range(first, near_n):
            origin = side * near_n + (z % near_n + o) % near_n
            rows_copy(o, origin, origin).wait_recv()
            prepare(origin)
        activate(side)

    group = chans // 2
    line_of = lax.broadcasted_iota(jnp.int32, (half, LANES), 0)

    def cross(first):
        for q in range(outer):
            at = slice(chans * block + q * half, chans * block + (q + 1) * half)
            reals, imags = [], []
            for c in range(first, first + group):
                line = slice(c * block + q * half, c * block + (q + 1) * half)
                gr, gi = spec_back[line, re_l], spec_back[line, im_l]
                hr, hi_ = spec_hidden[line, re_l], spec_hidden[line, im_l]
                reals.append(gr * hr + gi * hi_)
                imags.append(gr * hi_ - gi * hr)
            for side, values in ((re_l, reals), (im_l, imags)):
                value = fold_rows(values)
                work[at, side] = value if first == 0 else jnp.where(line_of < group, work[at, side], value)

    for c in range(chans):
        values = [
            (hidden_ref[c * half : (c + 1) * half, cols(m)],
             hidden_ref[(chans + c) * half : (chans + c + 1) * half, cols(m)])
            for m in range(outer)]
        store_forward(spec_hidden, c * block, values)
        if c + 1 == group:
            multiply(spec_hidden, 0, group * block, tables_ref, 0)
    cross(0)
    multiply(spec_hidden, group * block, group * block, tables_ref, 0)
    cross(group)

    multiply(work, chans * block, block, tables_ref, 2)
    for m, (re, im) in enumerate(load_inverse(work, chans * block)):
        outgoing[m] = re

    def folded(value):
        return jnp.sum(value, axis=0, keepdims=True)

    def mate(o):
        oz, ok, oc = o // (team_k * ch_n), o // ch_n % team_k, o % ch_n
        there_z = z // team_z * team_z + (z + oz) % team_z
        there_k = k // team_k * team_k + (k + ok) % team_k
        return there_z, there_k, (c0 + oc) % ch_n

    def rank(at):
        return (at[0] % team_z * team_k + at[1] % team_k) * ch_n + at[2]

    def sum_copy(o):
        target = mate(o)
        return pltpu.make_async_remote_copy(
            src_ref=outgoing.at[pl.ds(rank(target) * per, per)], dst_ref=incoming.at[o],
            send_sem=sum_send, recv_sem=sum_recv,
            device_id=(slab, *target), device_id_type=MESH)

    each(team_n, lambda o: sum_copy(o).start())

    @pl.loop(0, chans)
    def _(c):
        for q in range(outer):
            tr, ti = tap_row(q, c)
            rows = pl.ds(start_of(c) + q * half, half)
            hr, hi_ = spec_hidden[rows, re_l], spec_hidden[rows, im_l]
            work[rows, re_l] = tr * hr + ti * hi_
            work[rows, im_l] = tr * hi_ - ti * hr

    for s in range(0, chans * block, step):
        multiply(work, s, step, tables_ref, 2)

    partial[...] = jnp.zeros(partial.shape, jnp.float32)

    @pl.loop(0, chans // 2)
    def _(c):
        for side, rows in enumerate((lo, hi)):
            at = pl.ds(pl.multiple_of(side * chans * half + c * both, both), both)
            at_high = pl.ds(pl.multiple_of(c * both, both), both)
            at_low = pl.ds(pl.multiple_of(chans * half + c * both, both), both)
            for m in range(outer):
                gate = gate_ref[at, cols(m)]
                grad = jnp.concatenate([back[2 * c, rows, cols(m)], back[2 * c + 1, rows, cols(m)]], axis=0)
                grad = grad * (gate + hidden_ref[at, cols(m)] * (1.0 - gate))
                high = grad.astype(jnp.bfloat16)
                grads_ref[side, at_high, cols(m)] = high
                grads_ref[side, at_low, cols(m)] = (grad - high.astype(jnp.float32)).astype(jnp.bfloat16)

    wide = masks_ref.shape[2]
    totals = []
    for side in range(2):
        total = lax.dot_general(
            grads_ref[side], lines_ref[side * depth : (side + 1) * depth, :], (((1,), (1,)), ((), ())),
            preferred_element_type=jnp.float32)
        total = total[0 : chans * half] + total[chans * half : 2 * chans * half]
        if wide > depth:
            total = jnp.concatenate([total, jnp.zeros((chans * half, wide - depth), jnp.float32)], axis=1)
        totals.append(total)
    for c in range(chans):
        values = []
        for t in range(10):
            value = totals[0][c * half : (c + 1) * half] * masks_ref[t, lo, :]
            value = value + totals[1][c * half : (c + 1) * half] * masks_ref[t, hi, :]
            values.append(functools.reduce(
                lambda x, y: x + y, [value[:, at : at + LANES] for at in range(0, wide, LANES)]))
        partial[c, 0:8, :] = fold_rows(values[0:8])
        partial[c, 8:9, :] = folded(values[8])
        partial[c, 9:10, :] = folded(values[9])

    @pl.loop(0, chans)
    def _(c):
        sums = [jnp.zeros((half, LANES), jnp.float32) for _ in range(9)]
        for m, (re, im) in enumerate(load_inverse(work, start_of(c))):
            filt[c, lo, cols(m)] = re
            filt[c, hi, cols(m)] = im
            for t in range(9):
                sums[t] = sums[t] + re * cot_shift[t, lo, cols(m)] + im * cot_shift[t, hi, cols(m)]
        for t in range(9):
            partial[c, 16 + t : 17 + t, :] = folded(sums[t])

    small = lax.dot_general(
        jnp.ones((8, LANES), jnp.float32), partial[...].reshape(chans * SLOTS, LANES),
        (((1,), (1,)), ((), ())),
        precision=lax.Precision.HIGHEST, preferred_element_type=jnp.float32)
    width = chans_dev * SLOTS
    for h in range(ch_n):
        small_own[h] = small[0:1, h * width : (h + 1) * width]

    mine = pl.multiple_of(rank((z, k, c0)) * per, per)
    total = outgoing[pl.ds(mine, per)]
    summed = incoming.at[pl.ds(1, team_n - 1)]
    all_of(summed, summed, sum_send, sum_recv).wait_recv()
    for o in range(1, team_n):
        total = total + incoming[o]
    used = per * chans_dev
    for h in range(ch_n):
        for p in range(per):
            at = slice(p * chans_dev, (p + 1) * chans_dev)
            spread[h, at, :] = total[p, h * chans_dev : (h + 1) * chans_dev]
        spread[h, used : used + 1, :] = small_own[h]
    spreads = gathered.at[pl.ds(0, n - 1), pl.ds(0, used + 1)]

    def gather_copy(o):
        target = partner(o)
        return pltpu.make_async_remote_copy(
            src_ref=spread.at[target[2], pl.ds(0, used + 1)], dst_ref=gathered.at[me, pl.ds(0, used + 1)],
            send_sem=gather_send, recv_sem=gather_recv,
            device_id=(slab, *target), device_id_type=MESH)

    each(n, lambda o: gather_copy(o).start())
    gathered[me] = spread[c0]

    @pl.loop(0, outer)
    def _(m):
        at = pl.ds(pl.multiple_of(m * LANES, LANES), LANES)
        for rows in (lo, hi):
            pieces = [filt[c, rows, at] for c in range(chans)]
            for t in range(9):
                total = second_ref[t // 3, t % 3, 0] * pieces[0]
                for c in range(1, chans):
                    total = total + second_ref[t // 3, t % 3, c] * pieces[c]
                mixed[t, rows, at] = total

    sides = []
    for j in range(3):
        total = mixed[3 + j]
        for i in (0, 2):
            total = total + pltpu.roll(mixed[3 * i + j], -(i - 1) * rq % both, 0)
        sides.append(total)
    image = sides[1] + from_left(sides[0]) + from_right(sides[2])
    for a in range(angles):
        sino_ref[a] = image[a * rq : (a + 1) * rq]

    if ang_n > 1:
        sent = got.at[pl.ds(0, ang_n - 1), pl.ds(0, (rq + 2) * outer)]
        all_of(sent, sent, rows_send, rows_recv.at[0]).wait_send()
    if ch_n > 1:
        sent = all_taps.at[pl.ds(0, ch_n - 1)]
        all_of(sent, sent, taps_send, taps_recv).wait_send()
        sent = all_packed.at[pl.ds(0, ch_n - 1)]
        all_of(sent, sent, packed_send, packed_recv).wait_send()

    @pl.when(sends_top)
    def _():
        top_copy(z).wait_send()

    @pl.when(sends_bottom)
    def _():
        bottom_copy(z).wait_send()

    all_of(summed, summed, sum_send, sum_recv).wait_send()

    all_of(spreads, spreads, gather_send, gather_recv).wait_recv()
    sums = gathered[0, used : used + 1, :]
    for d in range(1, n):
        sums = sums + gathered[d, used : used + 1, :]
    for l in range(chans_dev):
        for i in range(3):
            at = l * SLOTS + 3 * i
            first_out_ref[i, l : l + 1, :] = sums[:, at : at + 3]
            second_out_ref[i, l : l + 1, :] = sums[:, at + 16 : at + 19]
        bias_out_ref[0:1, l : l + 1] = sums[:, l * SLOTS + 9 : l * SLOTS + 10]

    for m in range(outer):
        owner, at = m // per, m % per
        rz, rk, rc = owner // (team_k * ch_n), owner // ch_n % team_k, owner % ch_n
        pieces = [
            gathered[number((jz + rz, jk + rk, rc)), at * chans_dev : (at + 1) * chans_dev, :]
            for jz in range(0, ang_n, team_z) for jk in range(0, row_n, team_k)]
        taps_out_ref[:, cols(m)] = functools.reduce(lambda x, y: x + y, pieces)

    all_of(spreads, spreads, gather_send, gather_recv).wait_send()


def deliver(*refs):
    count = (len(refs) - 1) // 2
    sources, targets, sems = refs[:count], refs[count : 2 * count], refs[-1]
    copies = [pltpu.make_async_copy(sources[at], targets[at], sems.at[at]) for at in range(count)]
    for copy in copies:
        copy.start()
    for copy in copies:
        copy.wait()


def on_device(sizes, tables, projections, conv1_weight, conv1_bias, filter_taps, conv2_weight, cotangent):
    ang_n, row_n, ch_n = sizes
    n = ang_n * row_n * ch_n
    _, held, columns = projections.shape
    chans_dev = conv1_weight.shape[0]
    chans = chans_dev * ch_n
    _, angles, rq, _ = cotangent.shape
    outer = columns // LANES
    both = angles * rq
    block = outer * both // 2
    rp = padded_rows(rq)
    team_n = math.prod(team_sizes(sizes)) * ch_n
    slot = -(-(outer // team_n * chans_dev + 1) // 8) * 8
    f32 = jnp.float32
    vmem = pl.BlockSpec(memory_space=pltpu.VMEM)
    hbm = pl.BlockSpec(memory_space=pltpu.HBM)
    dma = pltpu.SemaphoreType.DMA
    wide = (both, columns)
    shapes = (
        jax.ShapeDtypeStruct((angles, rq, columns), f32),
        jax.ShapeDtypeStruct((3, chans_dev, 3), f32),
        jax.ShapeDtypeStruct((1, chans_dev), f32),
        jax.ShapeDtypeStruct((chans_dev, columns), f32),
        jax.ShapeDtypeStruct((3, chans_dev, 3), f32),
    )
    results = pl.pallas_call(
        functools.partial(kernel, sizes),
        out_shape=tuple(pltpu.VMEM(leaf.shape, f32) for leaf in shapes),
        in_specs=[hbm] * 9,
        out_specs=(vmem,) * 5,
        scratch_shapes=[
            pltpu.VMEM((held, columns), f32),
            pltpu.VMEM((3, chans_dev, 3), f32),
            pltpu.VMEM((1, chans_dev), f32),
            pltpu.VMEM((chans_dev, columns), f32),
            pltpu.VMEM((angles, rq, columns), f32),
            pltpu.VMEM(tables[0].shape, jnp.bfloat16),
            pltpu.VMEM(tables[1].shape, f32),
            pltpu.VMEM(tables[2].shape, f32),
            pltpu.VMEM(((held + 2) * outer, LANES), f32),
            pltpu.VMEM((chans_dev, LANES), f32),
            pltpu.VMEM((ch_n, 1, LANES), f32),
            pltpu.VMEM((ang_n, rp * outer, LANES), f32),
            pltpu.VMEM((ang_n, outer, LANES), f32),
            pltpu.VMEM((ang_n, outer, LANES), f32),
            pltpu.VMEM((ch_n, chans_dev, columns), f32),
            pltpu.VMEM((ch_n, chans_dev, LANES), f32),
            pltpu.SMEM((ch_n, chans_dev, LANES), f32),
            pltpu.SMEM((3, 3, chans), f32),
            pltpu.VMEM((9,) + wide, f32),
            pltpu.VMEM((chans * block, 2 * LANES), f32),
            pltpu.VMEM((chans * block, 2 * LANES), f32),
            pltpu.VMEM((block, 2 * LANES), f32),
            pltpu.VMEM(((chans + 1) * block, 2 * LANES), f32),
            pltpu.VMEM((chans,) + wide, f32),
            pltpu.VMEM((chans * both, columns), f32),
            pltpu.VMEM((chans * both, columns), f32),
            pltpu.VMEM((chans,) + wide, f32),
            pltpu.VMEM((chans, SLOTS, LANES), f32),
            pltpu.VMEM((9,) + wide, f32),
            pltpu.VMEM((angles * 6 * rp, columns), jnp.bfloat16),
            pltpu.VMEM((2, chans * both, angles * 3 * rp), jnp.bfloat16),
            pltpu.VMEM((2, chans * both, columns), jnp.bfloat16),
            pltpu.VMEM((outer, chans, LANES), f32),
            pltpu.VMEM((team_n, outer // team_n, chans, LANES), f32),
            pltpu.VMEM((ch_n, slot, LANES), f32),
            pltpu.VMEM((n, slot, LANES), f32),
            dma(()), dma((ang_n,)), dma((2,)), dma((2,)),
            dma(()), dma(()), dma(()), dma(()),
            dma(()), dma(()), dma(()), dma(()), dma((9,)), dma(()),
        ],
        compiler_params=pltpu.CompilerParams(
            collective_id=0, has_side_effects=True, vmem_limit_bytes=63 * 2**20
        ),
        name="tomography",
    )(
        projections[0], jnp.transpose(conv1_weight, (1, 0, 2)), conv1_bias[None], filter_taps,
        jnp.transpose(conv2_weight, (1, 2, 0)), cotangent[0], *tables,
    )
    image, first, bias, taps_out, second = pl.pallas_call(
        deliver,
        out_shape=shapes,
        in_specs=[vmem] * 5,
        out_specs=(hbm,) * 5,
        scratch_shapes=[dma((5,))],
        name="deliver",
    )(*[pltpu.with_memory_space_constraint(leaf, pltpu.VMEM) for leaf in results])
    return (
        image[None], jnp.transpose(first, (1, 0, 2)), bias[0], taps_out,
        jnp.transpose(second, (1, 0, 2)),
    )


def solution(mesh):
    sizes = tuple(mesh.shape[axis] for axis in ("ang", "row", "ch"))

    def whole(projections, conv1_weight, conv1_bias, filter_taps, conv2_weight, cotangent):
        angles, rq = cotangent.shape[1], cotangent.shape[2] // (sizes[0] * sizes[2])
        tables = (*make_tables(projections.shape[-1]), make_masks(angles, rq))

        def local(*arrays):
            return on_device(sizes, tuple(jnp.asarray(t) for t in tables), *arrays)

        return jax.shard_map(
            local,
            mesh=mesh,
            in_specs=(
                P(("slab", "ang"), "row", None),
                P("ch", None, None),
                P("ch"),
                P("ch", None),
                P(),
                P(("slab", "row"), None, ("ang", "ch"), None),
            ),
            out_specs=(
                P(("slab", "row"), None, ("ang", "ch"), None),
                P(("slab", "ch"), None, None),
                P(("slab", "ch")),
                P(("slab", "ch"), None),
                P(("slab", "ch"), None, None),
            ),
            check_vma=False,
        )(projections, conv1_weight, conv1_bias, filter_taps, conv2_weight, cotangent)

    return whole
```
